128 devices in a mesh: freq: 8 (over y, core), trace: 16 (over x, z).
Axes of the slice: x: 4, y: 4, z: 4, core: 2. Of those that a mesh axis runs over, the one named last changes fastest.
Arguments:
- traces: bfloat16 [8, 4096, 4096], P('freq', 'trace'), may hold values from -6 to 6
- coords: int32 [4, 8, 4096], replicated, may hold values from 0 to 1023
- wavenumbers: int32 [4, 8, 4096], replicated, may hold values from 0 to 1023
- fold: int32 [8], replicated, may hold values from 512 to 4096, as said below
- selected: int32 [2, 8, 1024], P(None, None, 'freq'), may hold values from 0 to 4095
Outputs:
- spectrum: float32 [4096, 8, 2, 1024], P('trace', None, None, 'freq')
- coefficients: float32 [2, 8, 2, 1024], P(None, None, None, 'freq')
The draws below stay inside these ranges and needn't reach their ends.
Inputs may be any that keep to these rules, and one draw needn't show every extreme that they name: Slots 0 to fold - 1 of a patch are live, the rest are not; some patch has all 4096 slots live.
All inputs are finite; a program needn't handle non-finite values.
Results may differ from the reference program's by a relative error of at most 0.0052.
Values may be sent and summed in bfloat16 or wider, within the bound.
No kernel may reach another device: no remote copies, remote signals or barrier semaphores. Data moves between devices by JAX's collectives and lax.ppermute only.
A program may use at most 128 MiB of HBM per device.

```python
import math
import jax
import jax.numpy as jnp
from jax import lax

NT = 4096
NF = 1024
NK = 4096
GRID = 1024
ITERS = 2
PATCHES = 8
FOLD = 4096


def draw_fold(key, part):
    first = jax.random.fold_in(key, 11)
    second = jax.random.fold_in(key, 23)
    base = jax.random.randint(first, (PATCHES,), FOLD // 8, FOLD + 1)
    fullest = jax.random.randint(second, (), 0, PATCHES)
    return jnp.where(jnp.arange(PATCHES, dtype=jnp.int32) == fullest, FOLD, base).astype(jnp.int32)


def plant(drawn, rng, low, top_value):
    shape = drawn.shape
    spot = [jax.random.randint(jax.random.fold_in(rng, axis), (), 0, shape[axis]) for axis in range(len(shape))]
    drawn = drawn.at[tuple(spot)].set(low)
    longest = shape.index(max(shape))
    spot[longest] = (spot[longest] + 1) % shape[longest]
    return drawn.at[tuple(spot)].set(top_value)


def block_levels(key, extent, pieces, smallest, top_value):
    loudness, own = 1.0, jax.random.fold_in(key, 6)
    for dim, blocks in pieces:
        steps = jnp.exp(jax.random.uniform(jax.random.fold_in(own, dim), (blocks,), jnp.float32, smallest / len(pieces), top_value / len(pieces)))
        loudness = loudness * jnp.repeat(steps, extent[dim] // blocks).reshape([-1 if axis == dim else 1 for axis in range(len(extent))])
    return loudness


def scatter_about(key, shape, scale, bound, pieces=(), held_as=jnp.bfloat16):
    factor_of = block_levels(key, shape, pieces, -0.22, 0.18) if pieces else 1.0
    entries = jax.random.normal(key, shape, jnp.float32) * scale * factor_of
    return jnp.minimum(jnp.maximum(entries, -bound), bound).astype(held_as)


def setup_inputs(seed: int = 0) -> dict:
    seeds = jax.random.split(jax.random.key(seed), 6)
    return {
        "traces": scatter_about(seeds[0], (PATCHES, FOLD, NT), 1.0, 6.0, ((0, 8), (1, 16))),
        "coords": plant(jax.random.randint(seeds[1], (4, PATCHES, FOLD), 0, GRID), jax.random.fold_in(seeds[1], 1), 0, GRID - 1).astype(jnp.int32),
        "wavenumbers": plant(jax.random.randint(seeds[2], (4, PATCHES, NK), 0, GRID), jax.random.fold_in(seeds[2], 1), 0, GRID - 1).astype(jnp.int32),
        "fold": draw_fold(jax.random.fold_in(seeds[5], 71), 0),
        "selected": plant(jax.random.randint(seeds[4], (ITERS, PATCHES, NF), 0, NK), jax.random.fold_in(seeds[4], 1), 0, NK - 1).astype(jnp.int32),
    }


def dft_table(length, count):
    sample = jnp.arange(length, dtype=jnp.int32)
    bins = jnp.arange(count, dtype=jnp.int32)
    product = (sample[:, None] * bins[None, :]) % length
    angle = product.astype(jnp.float32) * (2.0 * math.pi / length)
    return jnp.concatenate([jnp.cos(angle), -jnp.sin(angle)], axis=1).astype(jnp.bfloat16)


def one_patch(inputs):
    rows, places, waves = inputs
    inner = jnp.zeros((waves.shape[1], places.shape[1]), jnp.int32)
    for comp in range(4):
        inner = inner + waves[comp][:, None] * places[comp][None, :]
    inner = inner % GRID
    angle = inner.astype(jnp.float32) * (2.0 * math.pi / GRID)
    atoms = jnp.concatenate([jnp.cos(angle), jnp.sin(angle)], axis=0).astype(jnp.bfloat16)
    product = jnp.dot(atoms, rows, preferred_element_type=jnp.float32)
    cand = waves.shape[1]
    s_real = product[:cand, :NF] + product[cand:, NF:]
    s_imag = product[:cand, NF:] - product[cand:, :NF]
    return jnp.stack([s_real, s_imag], axis=1)


def reference(traces, coords, wavenumbers, fold, selected):
    patches, slots, length = traces.shape
    table = dft_table(length, NF)
    spectra = jnp.dot(traces.reshape(patches * slots, length), table, preferred_element_type=jnp.float32)
    spectra = spectra.astype(jnp.bfloat16).reshape(patches, slots, 2, NF)
    live = (jnp.arange(slots, dtype=jnp.int32)[None, :] < fold[:, None]).astype(jnp.float32)
    res_real = spectra[:, :, 0, :].astype(jnp.float32) * live[:, :, None]
    res_imag = spectra[:, :, 1, :].astype(jnp.float32) * live[:, :, None]
    inverse = 1.0 / fold.astype(jnp.float32)
    gathered = []
    for iteration in range(ITERS):
        chosen = selected[iteration].astype(jnp.int32)
        picked = jnp.take_along_axis(wavenumbers, jnp.broadcast_to(chosen[None], (4,) + chosen.shape), axis=2)
        inner = jnp.zeros((patches, slots, NF), jnp.int32)
        for comp in range(4):
            inner = inner + picked[comp][:, None, :] * coords[comp][:, :, None]
        inner = inner % GRID
        angle = inner.astype(jnp.float32) * (2.0 * math.pi / GRID)
        cosine = jnp.cos(angle)
        sine = jnp.sin(angle)
        coef_real = jnp.sum(res_real * cosine + res_imag * sine, axis=1) * inverse[:, None]
        coef_imag = jnp.sum(res_imag * cosine - res_real * sine, axis=1) * inverse[:, None]
        mask = live[:, :, None]
        res_real = res_real - mask * (coef_real[:, None, :] * cosine - coef_imag[:, None, :] * sine)
        res_imag = res_imag - mask * (coef_real[:, None, :] * sine + coef_imag[:, None, :] * cosine)
        gathered.append(jnp.stack([coef_real, coef_imag], axis=1))
    rounded = jnp.concatenate([res_real, res_imag], axis=2).astype(jnp.bfloat16)
    spectrum = lax.map(one_patch, (rounded, jnp.moveaxis(coords, 1, 0), jnp.moveaxis(wavenumbers, 1, 0)))
    spectrum = jnp.moveaxis(spectrum, 0, 1)
    return (spectrum, jnp.stack(gathered, axis=0))
```

```python
import math

import jax
import jax.numpy as jnp
from jax import lax
from jax.experimental import pallas as pl
from jax.experimental.pallas import tpu as pltpu
from jax.sharding import Mesh
from jax.sharding import PartitionSpec as P

BF = jnp.bfloat16
F32 = jnp.float32
NT = 4096
SLOTS = 4096
GRID = 1024
TRACE = ("half", "xl", "z")
EIGHT = ("xl", "z")
ROUND = 12582912.0
R2 = math.sqrt(2.0)
VMEM = 58 << 20


def dot(a, b):
    return jnp.dot(a, b, preferred_element_type=F32)


def to_turn(t):
    return t - ((t + ROUND) - ROUND)


def cos_sin(r):
    y = r * r
    s = r * (
        R2 * 3.14159258
        + y * (R2 * -5.16770688 + y * (R2 * 2.55003138 + y * (R2 * -0.59804517 + y * (R2 * 0.07722012))))
    )
    c = R2 * 0.99999995 + y * (
        R2 * -4.93479286 + y * (R2 * 4.05841192 + y * (R2 * -1.33188016 + y * (R2 * 0.2196968)))
    )
    return 1.0 - s * s, s * c


def cos_sin_short(r):
    y = r * r
    s = r * (R2 * 3.14158202 + y * (R2 * -5.16714279 + y * (R2 * 2.541899 + y * (R2 * -0.55463613))))
    c = R2 * 0.9999933 + y * (R2 * -4.93393802 + y * (R2 * 4.04128385 + y * (R2 * -1.22212706)))
    return 1.0 - s * s, s * c


def low_high(v):
    high = v >> 5
    return (v & 31).astype(F32), high.astype(F32)


def wave_rows(w):
    low, high = low_high(w)
    return jnp.concatenate([high * (1 / 32), low * (1 / 32), low * (1 / 1024), jnp.zeros_like(low)], axis=0)


def place_rows(x):
    low, high = low_high(x)
    return jnp.concatenate([low, high, low, jnp.zeros_like(low)], axis=0)


def dft(traces, part):
    def body(x_ref, o_ref):
        f = pl.program_id(0) * 256 + lax.broadcasted_iota(jnp.int32, (64, 256), 1)
        n = lax.broadcasted_iota(jnp.int32, (64, 256), 0)

        def table(step):
            m = (n * f * step) & (NT - 1)
            m = jnp.where(m >= NT // 2, m - NT, m)
            return cos_sin(m.astype(F32) * (1.0 / NT))

        c_far, s_far = table(64)
        c_near, s_near = table(1)
        acc = jnp.zeros((256, 256), F32)
        for chunk in range(NT // 256):
            rows = []
            for a in range(chunk * 4, chunk * 4 + 4):
                ca, sa = c_far[a : a + 1, :], s_far[a : a + 1, :]
                if part == 0:
                    rows.append(ca * c_near - sa * s_near)
                else:
                    rows.append(-(sa * c_near) - ca * s_near)
            acc = acc + dot(x_ref[:, chunk * 256 : (chunk + 1) * 256], jnp.concatenate(rows, axis=0).astype(BF))
        o_ref[0] = acc[:, :128].astype(BF)
        o_ref[1] = acc[:, 128:].astype(BF)

    return pl.pallas_call(
        body,
        grid=(4,),
        out_shape=jax.ShapeDtypeStruct((8, 256, 128), BF),
        in_specs=[pl.BlockSpec((256, NT), lambda i: (0, 0))],
        out_specs=pl.BlockSpec((2, 256, 128), lambda i: (i, 0, 0)),
        compiler_params=pltpu.CompilerParams(vmem_limit_bytes=VMEM),
        cost_estimate=pl.CostEstimate(flops=2 * 256 * NT * 1024, bytes_accessed=3 << 20, transcendentals=0),
        name="dft" + str(part),
    )(traces)


def make_atoms(waves, places):
    rows = 256

    def body(w_ref, x_ref, o_ref):
        w = jnp.transpose(wave_rows(w_ref[...])).astype(BF)
        x = place_rows(x_ref[...]).astype(BF)
        for j in range(16):
            c, s = cos_sin_short(to_turn(dot(w, x[:, j * 256 : (j + 1) * 256])))
            o_ref[:, j * 256 : (j + 1) * 256] = c.astype(BF)
            o_ref[:, SLOTS + j * 256 : SLOTS + (j + 1) * 256] = s.astype(BF)

    count = waves.shape[1]
    return pl.pallas_call(
        body,
        grid=(count // rows,),
        out_shape=jax.ShapeDtypeStruct((count, 2 * SLOTS), BF),
        in_specs=[pl.BlockSpec((4, rows), lambda i: (0, i)), pl.BlockSpec((4, SLOTS), lambda i: (0, 0))],
        out_specs=pl.BlockSpec((rows, 2 * SLOTS), lambda i: (i, 0)),
        compiler_params=pltpu.CompilerParams(vmem_limit_bytes=VMEM),
        cost_estimate=pl.CostEstimate(flops=30 << 30, bytes_accessed=count * 16384, transcendentals=0),
        name="atoms",
    )(waves, places)


def pursue(real, imag, places, waves, chosen, fold):
    blocks, size = 16, 256

    def body(fold_ref, re_ref, im_ref, x_ref, w_ref, ch_ref, o_ref, co_ref, ec_ref, es_ref):
        table3 = w_ref[0] + w_ref[1] * 1024 + w_ref[2] * (1 << 20)
        index = jnp.concatenate([ch_ref[...]] * 4, axis=0)
        low, high = index & 127, index >> 7
        found3 = jnp.zeros((8, 128), jnp.int32)
        found1 = jnp.zeros((8, 128), jnp.int32)
        for r in range(32):
            here = high == r
            g3 = jnp.take_along_axis(jnp.broadcast_to(table3[r : r + 1], (8, 128)), low, axis=1)
            g1 = jnp.take_along_axis(jnp.broadcast_to(w_ref[3, r : r + 1], (8, 128)), low, axis=1)
            found3 = jnp.where(here, g3, found3)
            found1 = jnp.where(here, g1, found1)
        parts = [found3 & 1023, (found3 >> 10) & 1023, found3 >> 20, found1]
        picked = jnp.concatenate(
            [jnp.concatenate([v[t : t + 1] for v in parts], axis=0) for t in range(2)], axis=1
        )
        w = wave_rows(picked).astype(BF)
        count = fold_ref[0]
        inverse = 1.0 / count.astype(F32)
        zero = jnp.zeros((8, 128), F32)

        def fold8(v):
            return jnp.sum(v.reshape(size // 8, 8, 128), axis=0)

        def gather(j, sums):
            start = pl.multiple_of(j * size, size)
            rows = pl.ds(start, size)
            x = jnp.transpose(place_rows(x_ref[:, rows])).astype(BF)
            c, s = cos_sin(to_turn(dot(x, w)))
            ec_ref[rows, :] = c
            es_ref[rows, :] = s
            live = (start + lax.broadcasted_iota(jnp.int32, (size, 128), 0)) < count
            re = jnp.where(live, re_ref[rows, :].astype(F32), 0.0)
            im = jnp.where(live, im_ref[rows, :].astype(F32), 0.0)
            c0, c1, s0, s1 = c[:, :128], c[:, 128:], s[:, :128], s[:, 128:]
            new = (
                re * c0 + im * s0,
                im * c0 - re * s0,
                re * c1 + im * s1,
                im * c1 - re * s1,
                jnp.where(live, c0 * c1 + s0 * s1, 0.0),
                jnp.where(live, s0 * c1 - c0 * s1, 0.0),
            )
            return tuple(a + fold8(b) for a, b in zip(sums, new))

        sums = lax.fori_loop(0, blocks, gather, (zero,) * 6)
        r0, i0, r1, i1, gr, gi = [jnp.sum(v, axis=0, keepdims=True) for v in sums]
        a0, b0 = r0 * inverse, i0 * inverse
        a1 = (r1 - (a0 * gr - b0 * gi)) * inverse
        b1 = (i1 - (a0 * gi + b0 * gr)) * inverse

        def split(v):
            first = v.astype(BF).astype(F32)
            second = (v - first).astype(BF).astype(F32)
            return [first, second, v - first - second]

        packed = [jnp.concatenate(pair, axis=1) for pair in zip(split(a0), split(b0))]
        packed += [jnp.concatenate(pair, axis=1) for pair in zip(split(a1), split(b1))]
        co_ref[...] = jnp.concatenate(packed + [jnp.zeros((10, 256), F32)], axis=0).astype(BF)

        def subtract(j, carry):
            start = pl.multiple_of(j * size, size)
            rows = pl.ds(start, size)
            c, s = ec_ref[rows, :], es_ref[rows, :]
            live = (start + lax.broadcasted_iota(jnp.int32, (size, 128), 0)) < count
            c0, c1, s0, s1 = c[:, :128], c[:, 128:], s[:, :128], s[:, 128:]
            re = re_ref[rows, :].astype(F32) - (a0 * c0 - b0 * s0) - (a1 * c1 - b1 * s1)
            im = im_ref[rows, :].astype(F32) - (a0 * s0 + b0 * c0) - (a1 * s1 + b1 * c1)
            re = jnp.where(live, re, 0.0)
            im = jnp.where(live, im, 0.0)
            o_ref[0, rows, :128] = re.astype(BF)
            o_ref[0, rows, 128:] = im.astype(BF)
            o_ref[1, rows, :128] = im.astype(BF)
            o_ref[1, rows, 128:] = (-re).astype(BF)
            return carry

        lax.fori_loop(0, blocks, subtract, 0)

    whole = pl.BlockSpec(memory_space=pltpu.VMEM)
    return pl.pallas_call(
        body,
        out_shape=(jax.ShapeDtypeStruct((2, SLOTS, 256), BF), jax.ShapeDtypeStruct((16, 256), BF)),
        in_specs=[pl.BlockSpec(memory_space=pltpu.SMEM)] + [whole] * 5,
        out_specs=(whole, whole),
        scratch_shapes=[pltpu.VMEM((SLOTS, 256), F32), pltpu.VMEM((SLOTS, 256), F32)],
        compiler_params=pltpu.CompilerParams(vmem_limit_bytes=VMEM),
        cost_estimate=pl.CostEstimate(flops=6 << 30, bytes_accessed=6 << 20, transcendentals=0),
        name="pursue",
    )(fold, real, imag, places, waves, chosen)


def project(atoms, residual, extra, first):
    tall = 144 if extra is not None else 128

    def body(a_ref, r_ref, *rest):
        o_ref = rest[-1]
        acc = dot(a_ref[:, :SLOTS], r_ref[0]) + dot(a_ref[:, SLOTS:], r_ref[1])
        for b in range(4):
            o_ref[b, :128, :] = acc[b * 128 : (b + 1) * 128].astype(BF)
            if extra is not None:
                o_ref[b, 128:, :] = rest[0][...]

    more = [] if extra is None else [extra]
    return pl.pallas_call(
        body,
        grid=(2,),
        out_shape=jax.ShapeDtypeStruct((8, tall, 256), BF),
        in_specs=[
            pl.BlockSpec((512, 2 * SLOTS), lambda i: (i + first, 0)),
            pl.BlockSpec((2, SLOTS, 256), lambda i: (0, 0, 0)),
        ]
        + [pl.BlockSpec((16, 256), lambda i: (0, 0))] * len(more),
        out_specs=pl.BlockSpec((4, tall, 256), lambda i: (i, 0, 0)),
        compiler_params=pltpu.CompilerParams(vmem_limit_bytes=VMEM),
        cost_estimate=pl.CostEstimate(flops=2 * 1024 * 8192 * 256, bytes_accessed=22 << 20, transcendentals=0),
        name="project" + str(first),
    )(atoms, residual, *more)


def finish(first, second):
    step = 32

    def body(a_ref, b_ref, e_ref, o_ref, c_ref):
        for p in range(8):
            for part in range(2):
                lanes = pl.ds(part * 128, 128)
                spread = pl.ds(2 * p + part, step, stride=16)
                o_ref[0, spread, :] = a_ref[p, :, lanes].astype(F32)
                o_ref[1, spread, :] = b_ref[p, :, lanes].astype(F32)

        @pl.when(pl.program_id(0) == 0)
        def _():
            for p in range(8):
                v = e_ref[p].astype(F32)
                for t in range(2):
                    total = v[3 * t : 3 * t + 1] + (v[3 * t + 1 : 3 * t + 2] + v[3 * t + 2 : 3 * t + 3])
                    row = t * 16 + 2 * p
                    c_ref[row : row + 1, :] = total[:, :128]
                    c_ref[row + 1 : row + 2, :] = total[:, 128:]

    return pl.pallas_call(
        body,
        grid=(128 // step,),
        out_shape=(jax.ShapeDtypeStruct((2, 2048, 128), F32), jax.ShapeDtypeStruct((32, 128), F32)),
        in_specs=[
            pl.BlockSpec((8, step, 256), lambda i: (0, i, 0)),
            pl.BlockSpec((8, step, 256), lambda i: (0, i, 0)),
            pl.BlockSpec((8, 16, 256), lambda i: (0, 8, 0)),
        ],
        out_specs=(
            pl.BlockSpec((2, step * 16, 128), lambda i: (0, i, 0)),
            pl.BlockSpec((32, 128), lambda i: (0, 0)),
        ),
        compiler_params=pltpu.CompilerParams(vmem_limit_bytes=VMEM),
        cost_estimate=pl.CostEstimate(flops=1 << 20, bytes_accessed=3 << 20, transcendentals=0),
        name="finish",
    )(first, second, first)


def local(traces, coords, wavenumbers, fold, selected):
    patch = lax.axis_index(EIGHT)
    half = lax.axis_index("half")
    places = lax.dynamic_slice_in_dim(coords, patch, 1, 1)[:, 0]
    waves = lax.dynamic_slice_in_dim(wavenumbers, patch, 1, 1)[:, 0]
    chosen = lax.dynamic_slice_in_dim(selected, patch, 1, 1)[:, 0]
    count = lax.dynamic_slice_in_dim(fold, patch, 1, 0)
    mine = lax.dynamic_slice_in_dim(waves, half * 2048, 2048, 1)
    mine = mine.reshape(4, 8, 2, 128).transpose(0, 2, 1, 3).reshape(4, 2048)

    received = []
    for part in range(2):
        sent = dft(traces[0], part)
        moved = lax.all_to_all(sent, "freq", split_axis=0, concat_axis=0, tiled=True)
        both = jnp.concatenate([moved, moved], axis=0)
        moved = lax.all_to_all(both, TRACE, split_axis=0, concat_axis=0, tiled=True)
        received.append(moved.reshape(SLOTS, 128))
    atoms = make_atoms(mine, places)
    residual, coefs = pursue(received[0], received[1], places, waves.reshape(4, 32, 128), chosen, count)
    first = lax.all_to_all(project(atoms, residual, coefs, 0), EIGHT, split_axis=0, concat_axis=0, tiled=True)
    second = lax.all_to_all(project(atoms, residual, None, 2), EIGHT, split_axis=0, concat_axis=0, tiled=True)
    spectrum, coefficients = finish(first, second)
    return spectrum.reshape(256, 8, 2, 128), coefficients.reshape(2, 8, 2, 128)


def solution(mesh):
    split = Mesh(mesh.devices.reshape(8, 2, 2, 4), ("freq",) + TRACE)
    return jax.shard_map(
        local,
        mesh=split,
        in_specs=(P("freq", TRACE, None), P(), P(), P(), P(None, None, "freq")),
        out_specs=(P(TRACE, None, None, "freq"), P(None, None, None, "freq")),
        check_vma=False,
    )
```

```python
import math

import jax
import jax.numpy as jnp
from jax import lax
from jax.experimental import pallas as pl
from jax.experimental.pallas import tpu as pltpu
from jax.sharding import Mesh
from jax.sharding import PartitionSpec as P


BF = jnp.bfloat16
F32 = jnp.float32
NT = 4096
SLOTS = 4096
TRACE = ("half", "xl", "z")
EIGHT = ("xl", "z")
ROUND = 12582912.0
R2 = math.sqrt(2.0)
VMEM = 62 << 20
EARLY = 1024


def dot(a, b):
    return jnp.dot(a, b, preferred_element_type=F32)


def to_turn(t):
    return t - ((t + ROUND) - ROUND)


def cos_sin(r):
    y = r * r
    s = r * (
        R2 * 3.14159258
        + y * (R2 * -5.16770688 + y * (R2 * 2.55003138 + y * (R2 * -0.59804517 + y * (R2 * 0.07722012))))
    )
    c = R2 * 0.99999995 + y * (
        R2 * -4.93479286 + y * (R2 * 4.05841192 + y * (R2 * -1.33188016 + y * (R2 * 0.2196968)))
    )
    return 1.0 - s * s, s * c


def cos_sin_short(r):
    y = r * r
    s = r * (R2 * 3.14158202 + y * (R2 * -5.16714279 + y * (R2 * 2.541899 + y * (R2 * -0.55463613))))
    c = R2 * 0.9999933 + y * (R2 * -4.93393802 + y * (R2 * 4.04128385 + y * (R2 * -1.22212706)))
    return 1.0 - s * s, s * c


def low_high(v):
    high = v >> 5
    return (v & 31).astype(F32), high.astype(F32)


def wave_rows(w):
    low, high = low_high(w)
    return jnp.concatenate([high * (1 / 32), low * (1 / 32), low * (1 / 1024), jnp.zeros_like(low)], axis=0)


def place_rows(x):
    low, high = low_high(x)
    return jnp.concatenate([low, high, low, jnp.zeros_like(low)], axis=0)


def patch_rows(ref, patch, start, size):
    return jnp.concatenate([ref[c, pl.ds(patch, 1), pl.ds(start, size)] for c in range(4)], axis=0)


def dft(traces):
    half = NT // 2

    def body(x_ref, o_ref):
        f = pl.program_id(0) * 128 + lax.broadcasted_iota(jnp.int32, (64, 128), 1)
        n = lax.broadcasted_iota(jnp.int32, (64, 128), 0)

        def table(step):
            m = (n * f * step) & (NT - 1)
            m = jnp.where(m >= half, m - NT, m)
            return cos_sin(m.astype(F32) * (1.0 / NT))

        c_far, s_far = table(64)
        c_near, s_near = table(1)
        acc = jnp.zeros((512, 256), F32)
        for chunk in range(half // 256):
            rows = []
            for a in range(chunk * 4, chunk * 4 + 4):
                ca, sa = c_far[a : a + 1, :], s_far[a : a + 1, :]
                real = (ca * c_near - sa * s_near).astype(BF)
                imag = (-(sa * c_near) - ca * s_near).astype(BF)
                rows.append(jnp.concatenate([real, imag], axis=1))
            low = x_ref[:, chunk * 256 : (chunk + 1) * 256]
            high = x_ref[:, half + chunk * 256 : half + (chunk + 1) * 256]
            acc = acc + dot(jnp.concatenate([low, high], axis=0), jnp.concatenate(rows, axis=0))
        odd = (lax.broadcasted_iota(jnp.int32, (256, 256), 1) & 1) == 1
        o_ref[0] = jnp.where(odd, acc[:256] - acc[256:], acc[:256] + acc[256:]).astype(BF)

    return pl.pallas_call(
        body,
        grid=(8,),
        out_shape=jax.ShapeDtypeStruct((8, 256, 256), BF),
        in_specs=[pl.BlockSpec((256, NT), lambda i: (0, 0))],
        out_specs=pl.BlockSpec((1, 256, 256), lambda i: (i, 0, 0)),
        compiler_params=pltpu.CompilerParams(vmem_limit_bytes=VMEM),
        cost_estimate=pl.CostEstimate(flops=2 * 256 * NT * 2048, bytes_accessed=3 << 20, transcendentals=0),
        name="dft",
    )(traces)


def make_atoms(waves, places, first, count):
    rows = 256

    def body(w_ref, x_ref, o_ref):
        patch = lax.axis_index("xl") * 4 + lax.axis_index("z")
        start = lax.axis_index("half") * 2048 + first + pl.program_id(0) * rows
        start = pl.multiple_of(start, rows)
        w = jnp.transpose(wave_rows(patch_rows(w_ref, patch, start, rows))).astype(BF)
        x = place_rows(patch_rows(x_ref, patch, 0, SLOTS)).astype(BF)
        for j in range(16):
            c, s = cos_sin_short(to_turn(dot(w, x[:, j * 256 : (j + 1) * 256])))
            o_ref[:, j * 256 : (j + 1) * 256] = c.astype(BF)
            o_ref[:, SLOTS + j * 256 : SLOTS + (j + 1) * 256] = s.astype(BF)

    whole = pl.BlockSpec((4, 8, 4096), lambda i: (0, 0, 0))
    return pl.pallas_call(
        body,
        grid=(count // rows,),
        out_shape=jax.ShapeDtypeStruct((count, 2 * SLOTS), BF),
        in_specs=[whole, whole],
        out_specs=pl.BlockSpec((rows, 2 * SLOTS), lambda i: (i, 0)),
        compiler_params=pltpu.CompilerParams(vmem_limit_bytes=VMEM),
        cost_estimate=pl.CostEstimate(flops=count * (15 << 20), bytes_accessed=count * 16384, transcendentals=0),
        name="atoms",
    )(waves, places)


def chosen_tables(places, waves, chosen, fold):
    size = 512

    def body(fold_ref, x_ref, w_ref, ch_ref, c_ref, s_ref, g_ref, pick_ref):
        patch = lax.axis_index("xl") * 4 + lax.axis_index("z")
        step = pl.program_id(0)

        @pl.when(step == 0)
        def _():
            rows = [w_ref[c, pl.ds(patch, 1), :] for c in range(4)]
            table3 = rows[0] + rows[1] * 1024 + rows[2] * (1 << 20)
            index = jnp.concatenate([ch_ref[t, pl.ds(patch, 1), :] for t in range(2)] * 4, axis=0)
            low, high = index & 127, index >> 7
            found3 = jnp.zeros((8, 128), jnp.int32)
            found1 = jnp.zeros((8, 128), jnp.int32)
            for r in range(32):
                here = high == r
                lanes = slice(r * 128, (r + 1) * 128)
                g3 = jnp.take_along_axis(jnp.broadcast_to(table3[:, lanes], (8, 128)), low, axis=1)
                g1 = jnp.take_along_axis(jnp.broadcast_to(rows[3][:, lanes], (8, 128)), low, axis=1)
                found3 = jnp.where(here, g3, found3)
                found1 = jnp.where(here, g1, found1)
            parts = [found3 & 1023, (found3 >> 10) & 1023, found3 >> 20, found1]
            picked = [jnp.concatenate([v[t : t + 1] for v in parts], axis=0) for t in range(2)]
            pick_ref[...] = wave_rows(jnp.concatenate(picked, axis=1)).astype(BF)
            g_ref[...] = jnp.zeros((16, 128), F32)

        start = pl.multiple_of(step * size, size)
        x = jnp.transpose(place_rows(patch_rows(x_ref, patch, start, size))).astype(BF)
        c, s = cos_sin(to_turn(dot(x, pick_ref[...])))
        c_ref[...] = c
        s_ref[...] = s
        live = (start + lax.broadcasted_iota(jnp.int32, (size, 128), 0)) < fold_ref[patch]
        c0, c1, s0, s1 = c[:, :128], c[:, 128:], s[:, :128], s[:, 128:]
        real = jnp.where(live, c0 * c1 + s0 * s1, 0.0)
        imag = jnp.where(live, s0 * c1 - c0 * s1, 0.0)
        g_ref[:8, :] += jnp.sum(real.reshape(size // 8, 8, 128), axis=0)
        g_ref[8:, :] += jnp.sum(imag.reshape(size // 8, 8, 128), axis=0)

    whole = pl.BlockSpec((4, 8, 4096), lambda i: (0, 0, 0))
    return pl.pallas_call(
        body,
        grid=(SLOTS // size,),
        out_shape=(
            jax.ShapeDtypeStruct((SLOTS, 256), F32),
            jax.ShapeDtypeStruct((SLOTS, 256), F32),
            jax.ShapeDtypeStruct((16, 128), F32),
        ),
        in_specs=[
            pl.BlockSpec(memory_space=pltpu.SMEM),
            whole,
            whole,
            pl.BlockSpec((2, 8, 128), lambda i: (0, 0, 0)),
        ],
        out_specs=(
            pl.BlockSpec((size, 256), lambda i: (i, 0)),
            pl.BlockSpec((size, 256), lambda i: (i, 0)),
            pl.BlockSpec((16, 128), lambda i: (0, 0)),
        ),
        scratch_shapes=[pltpu.VMEM((16, 256), BF)],
        compiler_params=pltpu.CompilerParams(vmem_limit_bytes=VMEM),
        cost_estimate=pl.CostEstimate(flops=4 << 30, bytes_accessed=9 << 20, transcendentals=0),
        name="tables",
    )(fold, places, waves, chosen)


def pursue(received, cosine, sine, cross, fold, atoms):
    size, blocks, tall = 128, 8, 512
    span = SLOTS // blocks
    parts = len(atoms)
    each = 2048 // parts

    def body(fold_ref, g_ref, r_hbm, c_hbm, s_hbm, *rest):
        a_hbm, (o_ref, r_ref, c_ref, s_ref, a_ref, z_ref, sem, a_sem) = rest[:parts], rest[parts:]
        patch = lax.axis_index("xl") * 4 + lax.axis_index("z")
        loads = []
        for j in range(blocks):
            rows = pl.ds(j * span, span)
            trio = [
                pltpu.make_async_copy(src.at[rows, :], dst.at[rows, :], sem.at[j, k])
                for k, (src, dst) in enumerate([(r_hbm, r_ref), (c_hbm, c_ref), (s_hbm, s_ref)])
            ]
            for copy in trio:
                copy.start()
            loads.append(trio)
        streams = []
        for m in range(2048 // tall):
            piece, offset = divmod(m * tall, each)
            copy = pltpu.make_async_copy(
                a_hbm[piece].at[pl.ds(offset, tall), :], a_ref.at[pl.ds(m * tall, tall), :], a_sem.at[m]
            )
            copy.start()
            streams.append(copy)

        count = fold_ref[patch]
        inverse = 1.0 / jnp.full((1, 128), count, jnp.int32).astype(F32)
        zero = jnp.zeros((8, 128), F32)
        row = lax.broadcasted_iota(jnp.int32, (size, 128), 0)

        def fold8(v):
            return jnp.sum(v.reshape(size // 8, 8, 128), axis=0)

        def gather(j, sums):
            start = pl.multiple_of(j * size, size)
            rows = pl.ds(start, size)
            live = row < count - start
            c0, c1 = c_ref[rows, :128], c_ref[rows, 128:]
            s0, s1 = s_ref[rows, :128], s_ref[rows, 128:]
            re = jnp.where(live, r_ref[rows, :128].astype(F32), 0.0)
            im = jnp.where(live, r_ref[rows, 128:].astype(F32), 0.0)
            new = (re * c0 + im * s0, im * c0 - re * s0, re * c1 + im * s1, im * c1 - re * s1)
            return tuple(a + fold8(b) for a, b in zip(sums, new))

        sums = (zero,) * 4
        for j in range(blocks):
            for copy in loads[j]:
                copy.wait()
            sums = lax.fori_loop(j * span // size, (j + 1) * span // size, gather, sums)
        r0, i0, r1, i1 = [jnp.sum(v, axis=0, keepdims=True) for v in sums]
        gr = jnp.sum(g_ref[:8, :], axis=0, keepdims=True)
        gi = jnp.sum(g_ref[8:, :], axis=0, keepdims=True)
        a0, b0 = r0 * inverse, i0 * inverse
        a1 = (r1 - (a0 * gr - b0 * gi)) * inverse
        b1 = (i1 - (a0 * gi + b0 * gr)) * inverse

        def split(v):
            first = v.astype(BF).astype(F32)
            second = (v - first).astype(BF).astype(F32)
            return [first, second, v - first - second]

        packed = [jnp.concatenate(pair, axis=1) for pair in zip(split(a0), split(b0))]
        packed += [jnp.concatenate(pair, axis=1) for pair in zip(split(a1), split(b1))]
        packed = jnp.concatenate(packed + [jnp.zeros((10, 256), F32)], axis=0).astype(BF)
        for b in range(8):
            o_ref[b, 256:, :] = packed

        def subtract(j, carry):
            start = pl.multiple_of(j * size, size)
            rows = pl.ds(start, size)
            live = row < count - start
            c0, c1 = c_ref[rows, :128], c_ref[rows, 128:]
            s0, s1 = s_ref[rows, :128], s_ref[rows, 128:]
            re = r_ref[rows, :128].astype(F32) - (a0 * c0 - b0 * s0) - (a1 * c1 - b1 * s1)
            im = r_ref[rows, 128:].astype(F32) - (a0 * s0 + b0 * c0) - (a1 * s1 + b1 * c1)
            re = jnp.where(live, re, 0.0).astype(BF)
            im = jnp.where(live, im, 0.0).astype(BF)
            z_ref[0, rows, :128] = re
            z_ref[0, rows, 128:] = im
            z_ref[1, rows, :128] = im
            z_ref[1, rows, 128:] = -re
            return carry

        lax.fori_loop(0, SLOTS // size, subtract, 0)

        for m in range(2048 // tall):
            streams[m].wait()
            rows = pl.ds(m * tall, tall)
            acc = dot(a_ref[rows, :SLOTS], z_ref[0]) + dot(a_ref[rows, SLOTS:], z_ref[1])
            for b in range(tall // 256):
                o_ref[m * (tall // 256) + b, :256, :] = acc[b * 256 : (b + 1) * 256].astype(BF)

    hbm = pl.BlockSpec(memory_space=pl.ANY)
    whole = pl.BlockSpec(memory_space=pltpu.VMEM)
    return pl.pallas_call(
        body,
        out_shape=jax.ShapeDtypeStruct((8, 272, 256), BF),
        in_specs=[pl.BlockSpec(memory_space=pltpu.SMEM), whole] + [hbm] * (3 + parts),
        out_specs=whole,
        scratch_shapes=[
            pltpu.VMEM((SLOTS, 256), BF),
            pltpu.VMEM((SLOTS, 256), F32),
            pltpu.VMEM((SLOTS, 256), F32),
            pltpu.VMEM((2048, 2 * SLOTS), BF),
            pltpu.VMEM((2, SLOTS, 256), BF),
            pltpu.SemaphoreType.DMA((blocks, 3)),
            pltpu.SemaphoreType.DMA((2048 // tall,)),
        ],
        compiler_params=pltpu.CompilerParams(vmem_limit_bytes=VMEM),
        cost_estimate=pl.CostEstimate(flops=9 << 30, bytes_accessed=45 << 20, transcendentals=0),
        name="pursue",
    )(fold, cross, received, cosine, sine, *atoms)


def finish(moved):
    step = 64

    def body(a_ref, e_ref, o_ref, c_ref):
        for p in range(8):
            for part in range(2):
                lanes = pl.ds(part * 128, 128)
                o_ref[pl.ds(2 * p + part, step, stride=16), :] = a_ref[p, :, lanes].astype(F32)

        @pl.when(pl.program_id(0) == 0)
        def _():
            for p in range(8):
                v = e_ref[p].astype(F32)
                for t in range(2):
                    total = v[3 * t : 3 * t + 1] + (v[3 * t + 1 : 3 * t + 2] + v[3 * t + 2 : 3 * t + 3])
                    row = t * 16 + 2 * p
                    c_ref[row : row + 1, :] = total[:, :128]
                    c_ref[row + 1 : row + 2, :] = total[:, 128:]

    return pl.pallas_call(
        body,
        grid=(256 // step,),
        out_shape=(jax.ShapeDtypeStruct((4096, 128), F32), jax.ShapeDtypeStruct((32, 128), F32)),
        in_specs=[
            pl.BlockSpec((8, step, 256), lambda i: (0, i, 0)),
            pl.BlockSpec((8, 16, 256), lambda i: (0, 16, 0)),
        ],
        out_specs=(
            pl.BlockSpec((step * 16, 128), lambda i: (i, 0)),
            pl.BlockSpec((32, 128), lambda i: (0, 0)),
        ),
        compiler_params=pltpu.CompilerParams(vmem_limit_bytes=VMEM),
        cost_estimate=pl.CostEstimate(flops=1 << 20, bytes_accessed=3 << 20, transcendentals=0),
        name="finish",
    )(moved, moved)


def local(traces, coords, wavenumbers, fold, selected):
    sent = dft(traces[0])
    moved = lax.all_to_all(sent, "freq", split_axis=0, concat_axis=0, tiled=True)
    both = jnp.concatenate([moved, moved], axis=0)
    moved = lax.all_to_all(both, TRACE, split_axis=0, concat_axis=0, tiled=True)
    early = make_atoms(wavenumbers, coords, 0, EARLY)
    late = make_atoms(wavenumbers, coords, EARLY, 2048 - EARLY)
    cosine, sine, cross = chosen_tables(coords, wavenumbers, selected, fold)
    sent = pursue(moved.reshape(SLOTS, 256), cosine, sine, cross, fold, [early, late])
    moved = lax.all_to_all(sent, EIGHT, split_axis=0, concat_axis=0, tiled=True)
    spectrum, coefficients = finish(moved)
    return spectrum.reshape(256, 8, 2, 128), coefficients.reshape(2, 8, 2, 128)


def solution(mesh):
    split = Mesh(mesh.devices.reshape(8, 2, 2, 4), ("freq",) + TRACE)
    return jax.shard_map(
        local,
        mesh=split,
        in_specs=(P("freq", TRACE, None), P(), P(), P(), P(None, None, "freq")),
        out_specs=(P(TRACE, None, None, "freq"), P(None, None, None, "freq")),
        check_vma=False,
    )
```

```python
import math

import jax
import jax.numpy as jnp
from jax import lax
from jax.experimental import pallas as pl
from jax.experimental.pallas import tpu as pltpu
from jax.sharding import Mesh
from jax.sharding import PartitionSpec as P


BF = jnp.bfloat16
F32 = jnp.float32
NT = 4096
SLOTS = 4096
TRACE = ("half", "xl", "z")
EIGHT = ("xl", "z")
ROUND = 12582912.0
R2 = math.sqrt(2.0)
VMEM = 62 << 20
EARLY = 1024


def dot(a, b):
    return jnp.dot(a, b, preferred_element_type=F32)


def to_turn(t):
    return t - ((t + ROUND) - ROUND)


def cos_sin(r):
    y = r * r
    s = r * (
        R2 * 3.14159258
        + y * (R2 * -5.16770688 + y * (R2 * 2.55003138 + y * (R2 * -0.59804517 + y * (R2 * 0.07722012))))
    )
    c = R2 * 0.99999995 + y * (
        R2 * -4.93479286 + y * (R2 * 4.05841192 + y * (R2 * -1.33188016 + y * (R2 * 0.2196968)))
    )
    return 1.0 - s * s, s * c


def cos_sin_short(r):
    y = r * r
    s = r * (R2 * 3.14158202 + y * (R2 * -5.16714279 + y * (R2 * 2.541899 + y * (R2 * -0.55463613))))
    c = R2 * 0.9999933 + y * (R2 * -4.93393802 + y * (R2 * 4.04128385 + y * (R2 * -1.22212706)))
    return 1.0 - s * s, s * c


def low_high(v):
    high = v >> 5
    return (v & 31).astype(F32), high.astype(F32)


def wave_rows(w):
    low, high = low_high(w)
    return jnp.concatenate([high * (1 / 32), low * (1 / 32), low * (1 / 1024), jnp.zeros_like(low)], axis=0)


def place_rows(x):
    low, high = low_high(x)
    return jnp.concatenate([low, high, low, jnp.zeros_like(low)], axis=0)


def patch_rows(ref, patch, start, size):
    return jnp.concatenate([ref[c, pl.ds(patch, 1), pl.ds(start, size)] for c in range(4)], axis=0)


def dft(traces):
    half = NT // 2
    width = 256

    def body(x_ref, o_ref):
        f = pl.program_id(0) * width + lax.broadcasted_iota(jnp.int32, (64, width), 1)
        n = lax.broadcasted_iota(jnp.int32, (64, width), 0)

        def table(step):
            m = (n * f * step) & (NT - 1)
            m = jnp.where(m >= half, m - NT, m)
            return cos_sin(m.astype(F32) * (1.0 / NT))

        c_far, s_far = table(64)
        c_near, s_near = table(1)
        acc = jnp.zeros((512, 2 * width), F32)
        for chunk in range(half // 256):
            rows = []
            for a in range(chunk * 4, chunk * 4 + 4):
                ca, sa = c_far[a : a + 1, :], s_far[a : a + 1, :]
                real = (ca * c_near - sa * s_near).astype(BF)
                imag = (-(sa * c_near) - ca * s_near).astype(BF)
                rows.append(jnp.concatenate([real, imag], axis=1))
            low = x_ref[:, chunk * 256 : (chunk + 1) * 256]
            high = x_ref[:, half + chunk * 256 : half + (chunk + 1) * 256]
            acc = acc + dot(jnp.concatenate([low, high], axis=0), jnp.concatenate(rows, axis=0))
        odd = (lax.broadcasted_iota(jnp.int32, (256, 2 * width), 1) & 1) == 1
        both = jnp.where(odd, acc[:256] - acc[256:], acc[:256] + acc[256:]).astype(BF)
        for g in range(width // 128):
            lanes = slice(g * 128, (g + 1) * 128)
            o_ref[g, :, :128] = both[:, :width][:, lanes]
            o_ref[g, :, 128:] = both[:, width:][:, lanes]

    return pl.pallas_call(
        body,
        grid=(1024 // width,),
        out_shape=jax.ShapeDtypeStruct((8, 256, 256), BF),
        in_specs=[pl.BlockSpec((256, NT), lambda i: (0, 0))],
        out_specs=pl.BlockSpec((width // 128, 256, 256), lambda i: (i, 0, 0)),
        compiler_params=pltpu.CompilerParams(vmem_limit_bytes=VMEM),
        cost_estimate=pl.CostEstimate(flops=2 * 256 * NT * 2048, bytes_accessed=3 << 20, transcendentals=0),
        name="dft",
    )(traces)


def make_atoms(waves, places, first, count):
    rows = 256

    def body(w_ref, x_ref, o_ref, place_ref):
        patch = lax.axis_index("xl") * 4 + lax.axis_index("z")

        @pl.when(pl.program_id(0) == 0)
        def _():
            place_ref[...] = place_rows(patch_rows(x_ref, patch, 0, SLOTS)).astype(BF)

        start = lax.axis_index("half") * 2048 + first + pl.program_id(0) * rows
        start = pl.multiple_of(start, rows)
        w = jnp.transpose(wave_rows(patch_rows(w_ref, patch, start, rows))).astype(BF)
        for j in range(16):
            c, s = cos_sin_short(to_turn(dot(w, place_ref[:, j * 256 : (j + 1) * 256])))
            o_ref[:, j * 256 : (j + 1) * 256] = c.astype(BF)
            o_ref[:, SLOTS + j * 256 : SLOTS + (j + 1) * 256] = s.astype(BF)

    whole = pl.BlockSpec((4, 8, 4096), lambda i: (0, 0, 0))
    return pl.pallas_call(
        body,
        grid=(count // rows,),
        out_shape=jax.ShapeDtypeStruct((count, 2 * SLOTS), BF),
        in_specs=[whole, whole],
        out_specs=pl.BlockSpec((rows, 2 * SLOTS), lambda i: (i, 0)),
        scratch_shapes=[pltpu.VMEM((16, SLOTS), BF)],
        compiler_params=pltpu.CompilerParams(vmem_limit_bytes=VMEM),
        cost_estimate=pl.CostEstimate(flops=count * (15 << 20), bytes_accessed=count * 16384, transcendentals=0),
        name="atoms",
    )(waves, places)


def chosen_tables(places, waves, chosen, fold):
    size = 512

    def body(fold_ref, x_ref, w_ref, ch_ref, c_ref, s_ref, g_ref, pick_ref):
        patch = lax.axis_index("xl") * 4 + lax.axis_index("z")
        step = pl.program_id(0)

        @pl.when(step == 0)
        def _():
            rows = [w_ref[c, pl.ds(patch, 1), :] for c in range(4)]
            table3 = rows[0] + rows[1] * 1024 + rows[2] * (1 << 20)
            index = jnp.concatenate([ch_ref[t, pl.ds(patch, 1), :] for t in range(2)] * 4, axis=0)
            low, high = index & 127, index >> 7
            found3 = jnp.zeros((8, 128), jnp.int32)
            found1 = jnp.zeros((8, 128), jnp.int32)
            for r in range(32):
                here = high == r
                lanes = slice(r * 128, (r + 1) * 128)
                g3 = jnp.take_along_axis(jnp.broadcast_to(table3[:, lanes], (8, 128)), low, axis=1)
                g1 = jnp.take_along_axis(jnp.broadcast_to(rows[3][:, lanes], (8, 128)), low, axis=1)
                found3 = jnp.where(here, g3, found3)
                found1 = jnp.where(here, g1, found1)
            parts = [found3 & 1023, (found3 >> 10) & 1023, found3 >> 20, found1]
            picked = [jnp.concatenate([v[t : t + 1] for v in parts], axis=0) for t in range(2)]
            pick_ref[...] = wave_rows(jnp.concatenate(picked, axis=1)).astype(BF)
            g_ref[...] = jnp.zeros((16, 128), F32)

        start = pl.multiple_of(step * size, size)
        x = jnp.transpose(place_rows(patch_rows(x_ref, patch, start, size))).astype(BF)
        c, s = cos_sin(to_turn(dot(x, pick_ref[...])))
        c_ref[...] = c
        s_ref[...] = s
        live = (start + lax.broadcasted_iota(jnp.int32, (size, 128), 0)) < fold_ref[patch]
        c0, c1, s0, s1 = c[:, :128], c[:, 128:], s[:, :128], s[:, 128:]
        real = jnp.where(live, c0 * c1 + s0 * s1, 0.0)
        imag = jnp.where(live, s0 * c1 - c0 * s1, 0.0)
        g_ref[:8, :] += jnp.sum(real.reshape(size // 8, 8, 128), axis=0)
        g_ref[8:, :] += jnp.sum(imag.reshape(size // 8, 8, 128), axis=0)

    whole = pl.BlockSpec((4, 8, 4096), lambda i: (0, 0, 0))
    return pl.pallas_call(
        body,
        grid=(SLOTS // size,),
        out_shape=(
            jax.ShapeDtypeStruct((SLOTS, 256), F32),
            jax.ShapeDtypeStruct((SLOTS, 256), F32),
            jax.ShapeDtypeStruct((16, 128), F32),
        ),
        in_specs=[
            pl.BlockSpec(memory_space=pltpu.SMEM),
            whole,
            whole,
            pl.BlockSpec((2, 8, 128), lambda i: (0, 0, 0)),
        ],
        out_specs=(
            pl.BlockSpec((size, 256), lambda i: (i, 0)),
            pl.BlockSpec((size, 256), lambda i: (i, 0)),
            pl.BlockSpec((16, 128), lambda i: (0, 0)),
        ),
        scratch_shapes=[pltpu.VMEM((16, 256), BF)],
        compiler_params=pltpu.CompilerParams(vmem_limit_bytes=VMEM),
        cost_estimate=pl.CostEstimate(flops=4 << 30, bytes_accessed=9 << 20, transcendentals=0),
        name="tables",
    )(fold, places, waves, chosen)


def pursue(received, cosine, sine, cross, fold, atoms):
    size, blocks, tall, ahead = 128, 8, 256, 3
    span = SLOTS // blocks
    parts = len(atoms)
    each = 2048 // parts

    def body(fold_ref, g_ref, r_hbm, c_hbm, s_hbm, *rest):
        a_hbm, (o_ref, r_ref, c_ref, s_ref, a_ref, z_ref, sem, a_sem) = rest[:parts], rest[parts:]
        patch = lax.axis_index("xl") * 4 + lax.axis_index("z")
        loads = []
        for j in range(blocks):
            rows = pl.ds(j * span, span)
            loads.append(
                [
                    pltpu.make_async_copy(src.at[rows, :], dst.at[rows, :], sem.at[j, k])
                    for k, (src, dst) in enumerate([(r_hbm, r_ref), (c_hbm, c_ref), (s_hbm, s_ref)])
                ]
            )
        for j in range(3):
            for copy in loads[j]:
                copy.start()

        def stream(m):
            piece, offset = divmod(m * tall, each)
            return pltpu.make_async_copy(
                a_hbm[piece].at[pl.ds(offset, tall), :], a_ref.at[pl.ds(m * tall, tall), :], a_sem.at[m]
            )

        count = fold_ref[patch]
        inverse = 1.0 / jnp.full((1, 128), count, jnp.int32).astype(F32)
        zero = jnp.zeros((8, 128), F32)
        row = lax.broadcasted_iota(jnp.int32, (size, 128), 0)

        def fold8(v):
            return jnp.sum(v.reshape(size // 8, 8, 128), axis=0)

        def gather(j, sums):
            start = pl.multiple_of(j * size, size)
            rows = pl.ds(start, size)
            live = row < count - start
            c0, c1 = c_ref[rows, :128], c_ref[rows, 128:]
            s0, s1 = s_ref[rows, :128], s_ref[rows, 128:]
            re = jnp.where(live, r_ref[rows, :128].astype(F32), 0.0)
            im = jnp.where(live, r_ref[rows, 128:].astype(F32), 0.0)
            new = (re * c0 + im * s0, im * c0 - re * s0, re * c1 + im * s1, im * c1 - re * s1)
            return tuple(a + fold8(b) for a, b in zip(sums, new))

        sums = (zero,) * 4
        for j in range(blocks):
            for copy in loads[j]:
                copy.wait()
            if j + 3 < blocks:
                for copy in loads[j + 3]:
                    copy.start()
            elif j + 3 < blocks + ahead:
                stream(j + 3 - blocks).start()
            sums = lax.fori_loop(j * span // size, (j + 1) * span // size, gather, sums)
        r0, i0, r1, i1 = [jnp.sum(v, axis=0, keepdims=True) for v in sums]
        gr = jnp.sum(g_ref[:8, :], axis=0, keepdims=True)
        gi = jnp.sum(g_ref[8:, :], axis=0, keepdims=True)
        a0, b0 = r0 * inverse, i0 * inverse
        a1 = (r1 - (a0 * gr - b0 * gi)) * inverse
        b1 = (i1 - (a0 * gi + b0 * gr)) * inverse

        def split(v):
            first = v.astype(BF).astype(F32)
            second = (v - first).astype(BF).astype(F32)
            return [first, second, v - first - second]

        packed = [jnp.concatenate(pair, axis=1) for pair in zip(split(a0), split(b0))]
        packed += [jnp.concatenate(pair, axis=1) for pair in zip(split(a1), split(b1))]
        packed = jnp.concatenate(packed + [jnp.zeros((10, 256), F32)], axis=0).astype(BF)
        for b in range(8):
            o_ref[b, 256:, :] = packed

        def subtract(j, carry):
            start = pl.multiple_of(j * size, size)
            rows = pl.ds(start, size)
            live = row < count - start
            c0, c1 = c_ref[rows, :128], c_ref[rows, 128:]
            s0, s1 = s_ref[rows, :128], s_ref[rows, 128:]
            re = r_ref[rows, :128].astype(F32) - (a0 * c0 - b0 * s0) - (a1 * c1 - b1 * s1)
            im = r_ref[rows, 128:].astype(F32) - (a0 * s0 + b0 * c0) - (a1 * s1 + b1 * c1)
            re = jnp.where(live, re, 0.0).astype(BF)
            im = jnp.where(live, im, 0.0).astype(BF)
            z_ref[0, rows, :128] = re
            z_ref[0, rows, 128:] = im
            z_ref[1, rows, :128] = im
            z_ref[1, rows, 128:] = -re
            return carry

        lax.fori_loop(0, SLOTS // size, subtract, 0)

        def project(m, carry):
            rows = pl.ds(pl.multiple_of(m * tall, tall), tall)
            pltpu.make_async_copy(a_ref.at[rows, :], a_ref.at[rows, :], a_sem.at[m]).wait()
            for later in range(ahead, 2048 // tall):

                @pl.when(m == later - ahead)
                def _(later=later):
                    stream(later).start()

            acc = dot(a_ref[rows, :SLOTS], z_ref[0]) + dot(a_ref[rows, SLOTS:], z_ref[1])
            o_ref[m, :256, :] = acc.astype(BF)
            return carry

        lax.fori_loop(0, 2048 // tall, project, 0)

    hbm = pl.BlockSpec(memory_space=pl.ANY)
    whole = pl.BlockSpec(memory_space=pltpu.VMEM)
    return pl.pallas_call(
        body,
        out_shape=jax.ShapeDtypeStruct((8, 272, 256), BF),
        in_specs=[pl.BlockSpec(memory_space=pltpu.SMEM), whole] + [hbm] * (3 + parts),
        out_specs=whole,
        scratch_shapes=[
            pltpu.VMEM((SLOTS, 256), BF),
            pltpu.VMEM((SLOTS, 256), F32),
            pltpu.VMEM((SLOTS, 256), F32),
            pltpu.VMEM((2048, 2 * SLOTS), BF),
            pltpu.VMEM((2, SLOTS, 256), BF),
            pltpu.SemaphoreType.DMA((blocks, 3)),
            pltpu.SemaphoreType.DMA((2048 // tall,)),
        ],
        compiler_params=pltpu.CompilerParams(vmem_limit_bytes=VMEM),
        cost_estimate=pl.CostEstimate(flops=9 << 30, bytes_accessed=45 << 20, transcendentals=0),
        name="pursue",
    )(fold, cross, received, cosine, sine, *atoms)


def finish(moved):
    step = 64

    def body(a_ref, e_ref, o_ref, c_ref):
        for p in range(8):
            for part in range(2):
                lanes = pl.ds(part * 128, 128)
                o_ref[pl.ds(2 * p + part, step, stride=16), :] = a_ref[p, :, lanes].astype(F32)

        @pl.when(pl.program_id(0) == 0)
        def _():
            for p in range(8):
                v = e_ref[p].astype(F32)
                for t in range(2):
                    total = v[3 * t : 3 * t + 1] + (v[3 * t + 1 : 3 * t + 2] + v[3 * t + 2 : 3 * t + 3])
                    row = t * 16 + 2 * p
                    c_ref[row : row + 1, :] = total[:, :128]
                    c_ref[row + 1 : row + 2, :] = total[:, 128:]

    return pl.pallas_call(
        body,
        grid=(256 // step,),
        out_shape=(jax.ShapeDtypeStruct((4096, 128), F32), jax.ShapeDtypeStruct((32, 128), F32)),
        in_specs=[
            pl.BlockSpec((8, step, 256), lambda i: (0, i, 0)),
            pl.BlockSpec((8, 16, 256), lambda i: (0, 16, 0)),
        ],
        out_specs=(
            pl.BlockSpec((step * 16, 128), lambda i: (i, 0)),
            pl.BlockSpec((32, 128), lambda i: (0, 0)),
        ),
        compiler_params=pltpu.CompilerParams(vmem_limit_bytes=VMEM),
        cost_estimate=pl.CostEstimate(flops=1 << 20, bytes_accessed=3 << 20, transcendentals=0),
        name="finish",
    )(moved, moved)


def local(traces, coords, wavenumbers, fold, selected):
    sent = dft(traces[0])
    moved = lax.all_to_all(sent, "freq", split_axis=0, concat_axis=0, tiled=True)
    both = jnp.concatenate([moved, moved], axis=0)
    moved = lax.all_to_all(both, TRACE, split_axis=0, concat_axis=0, tiled=True)
    early = make_atoms(wavenumbers, coords, 0, EARLY)
    late = make_atoms(wavenumbers, coords, EARLY, 2048 - EARLY)
    cosine, sine, cross = chosen_tables(coords, wavenumbers, selected, fold)
    sent = pursue(moved.reshape(SLOTS, 256), cosine, sine, cross, fold, [early, late])
    moved = lax.all_to_all(sent, EIGHT, split_axis=0, concat_axis=0, tiled=True)
    spectrum, coefficients = finish(moved)
    return spectrum.reshape(256, 8, 2, 128), coefficients.reshape(2, 8, 2, 128)


def solution(mesh):
    split = Mesh(mesh.devices.reshape(8, 2, 2, 4), ("freq",) + TRACE)
    return jax.shard_map(
        local,
        mesh=split,
        in_specs=(P("freq", TRACE, None), P(), P(), P(), P(None, None, "freq")),
        out_specs=(P(TRACE, None, None, "freq"), P(None, None, None, "freq")),
        check_vma=False,
    )
```

```python
import math

import jax
import jax.numpy as jnp
from jax import lax
from jax.experimental import pallas as pl
from jax.experimental.pallas import tpu as pltpu
from jax.sharding import Mesh
from jax.sharding import PartitionSpec as P


BF = jnp.bfloat16
F32 = jnp.float32
NT = 4096
SLOTS = 4096
TRACE = ("half", "xl", "z")
EIGHT = ("xl", "z")
ROUND = 12582912.0
R2 = math.sqrt(2.0)
VMEM = 62 << 20
EARLY = 896


def dot(a, b):
    return jnp.dot(a, b, preferred_element_type=F32)


def to_turn(t):
    return t - ((t + ROUND) - ROUND)


def cos_sin(r):
    y = r * r
    s = r * (
        R2 * 3.14159258
        + y * (R2 * -5.16770688 + y * (R2 * 2.55003138 + y * (R2 * -0.59804517 + y * (R2 * 0.07722012))))
    )
    c = R2 * 0.99999995 + y * (
        R2 * -4.93479286 + y * (R2 * 4.05841192 + y * (R2 * -1.33188016 + y * (R2 * 0.2196968)))
    )
    return 1.0 - s * s, s * c


def cos_sin_short(r):
    y = r * r
    s = r * (R2 * 3.14064003 + y * (R2 * -5.13690521 + y * (R2 * 2.29954682)))
    c = R2 * 0.9999933 + y * (R2 * -4.93393802 + y * (R2 * 4.04128385 + y * (R2 * -1.22212706)))
    return c * c - 1.0, s * c


def low_high(v):
    high = v >> 5
    return (v & 31).astype(F32), high.astype(F32)


def wave_rows(w):
    low, high = low_high(w)
    return jnp.concatenate([high * (1 / 32), low * (1 / 32), low * (1 / 1024), jnp.zeros_like(low)], axis=0)


def place_rows(x):
    low, high = low_high(x)
    return jnp.concatenate([low, high, low, jnp.zeros_like(low)], axis=0)


def patch_rows(ref, patch, start, size):
    return jnp.concatenate([ref[c, pl.ds(patch, 1), pl.ds(start, size)] for c in range(4)], axis=0)


def dft(traces):
    half = NT // 2
    width = 256

    def body(x_ref, o_ref):
        f = pl.program_id(0) * width + lax.broadcasted_iota(jnp.int32, (64, width), 1)
        n = lax.broadcasted_iota(jnp.int32, (64, width), 0)

        def table(step):
            m = (n * f * step) & (NT - 1)
            m = jnp.where(m >= half, m - NT, m)
            return cos_sin(m.astype(F32) * (1.0 / NT))

        c_far, s_far = table(64)
        c_near, s_near = table(1)
        acc = jnp.zeros((512, 2 * width), F32)
        for chunk in range(half // 256):
            rows = []
            for a in range(chunk * 4, chunk * 4 + 4):
                ca, sa = c_far[a : a + 1, :], s_far[a : a + 1, :]
                real = (ca * c_near - sa * s_near).astype(BF)
                imag = (-(sa * c_near) - ca * s_near).astype(BF)
                rows.append(jnp.concatenate([real, imag], axis=1))
            low = x_ref[:, chunk * 256 : (chunk + 1) * 256]
            high = x_ref[:, half + chunk * 256 : half + (chunk + 1) * 256]
            acc = acc + dot(jnp.concatenate([low, high], axis=0), jnp.concatenate(rows, axis=0))
        odd = (lax.broadcasted_iota(jnp.int32, (256, 2 * width), 1) & 1) == 1
        both = jnp.where(odd, acc[:256] - acc[256:], acc[:256] + acc[256:]).astype(BF)
        for g in range(width // 128):
            lanes = slice(g * 128, (g + 1) * 128)
            o_ref[g, :, :128] = both[:, :width][:, lanes]
            o_ref[g, :, 128:] = both[:, width:][:, lanes]

    return pl.pallas_call(
        body,
        grid=(1024 // width,),
        out_shape=jax.ShapeDtypeStruct((8, 256, 256), BF),
        in_specs=[pl.BlockSpec((256, NT), lambda i: (0, 0))],
        out_specs=pl.BlockSpec((width // 128, 256, 256), lambda i: (i, 0, 0)),
        compiler_params=pltpu.CompilerParams(vmem_limit_bytes=VMEM),
        cost_estimate=pl.CostEstimate(flops=2 * 256 * NT * 2048, bytes_accessed=3 << 20, transcendentals=0),
        name="dft",
    )(traces)


def make_atoms(waves, places, first, count):
    rows = 128

    def body(w_ref, x_ref, o_ref, place_ref, wave_ref):
        patch = lax.axis_index("xl") * 4 + lax.axis_index("z")

        @pl.when(pl.program_id(0) == 0)
        def _():
            place_ref[...] = place_rows(patch_rows(x_ref, patch, 0, SLOTS)).astype(BF)
            wave_ref[...] = wave_rows(patch_rows(w_ref, patch, 0, 4096))

        start = lax.axis_index("half") * 2048 + first + pl.program_id(0) * rows
        start = pl.multiple_of(start, rows)
        w = jnp.transpose(wave_ref[:, pl.ds(start, rows)]).astype(BF)
        for j in range(16):
            c, s = cos_sin_short(to_turn(dot(w, place_ref[:, j * 256 : (j + 1) * 256])))
            o_ref[:, j * 256 : (j + 1) * 256] = c.astype(BF)
            o_ref[:, SLOTS + j * 256 : SLOTS + (j + 1) * 256] = s.astype(BF)

    whole = pl.BlockSpec((4, 8, 4096), lambda i: (0, 0, 0))
    return pl.pallas_call(
        body,
        grid=(count // rows,),
        out_shape=jax.ShapeDtypeStruct((count, 2 * SLOTS), BF),
        in_specs=[whole, whole],
        out_specs=pl.BlockSpec((rows, 2 * SLOTS), lambda i: (i, 0)),
        scratch_shapes=[pltpu.VMEM((16, SLOTS), BF), pltpu.VMEM((16, 4096), F32)],
        compiler_params=pltpu.CompilerParams(vmem_limit_bytes=VMEM),
        cost_estimate=pl.CostEstimate(flops=count * (15 << 20), bytes_accessed=count * 16384, transcendentals=0),
        name="atoms",
    )(waves, places)


def chosen_tables(places, waves, chosen, fold):
    size = 512

    def body(fold_ref, x_ref, w_ref, ch_ref, c_ref, s_ref, g_ref, pick_ref):
        patch = lax.axis_index("xl") * 4 + lax.axis_index("z")
        step = pl.program_id(0)

        @pl.when(step == 0)
        def _():
            rows = [w_ref[c, pl.ds(patch, 1), :] for c in range(4)]
            table3 = rows[0] + rows[1] * 1024 + rows[2] * (1 << 20)
            index = jnp.concatenate([ch_ref[t, pl.ds(patch, 1), :] for t in range(2)] * 4, axis=0)
            low, high = index & 127, index >> 7
            found3 = jnp.zeros((8, 128), jnp.int32)
            found1 = jnp.zeros((8, 128), jnp.int32)
            for r in range(32):
                here = high == r
                lanes = slice(r * 128, (r + 1) * 128)
                g3 = jnp.take_along_axis(jnp.broadcast_to(table3[:, lanes], (8, 128)), low, axis=1)
                g1 = jnp.take_along_axis(jnp.broadcast_to(rows[3][:, lanes], (8, 128)), low, axis=1)
                found3 = jnp.where(here, g3, found3)
                found1 = jnp.where(here, g1, found1)
            parts = [found3 & 1023, (found3 >> 10) & 1023, found3 >> 20, found1]
            picked = [jnp.concatenate([v[t : t + 1] for v in parts], axis=0) for t in range(2)]
            pick_ref[...] = wave_rows(jnp.concatenate(picked, axis=1)).astype(BF)
            g_ref[...] = jnp.zeros((16, 128), F32)

        start = pl.multiple_of(step * size, size)
        x = jnp.transpose(place_rows(patch_rows(x_ref, patch, start, size))).astype(BF)
        c, s = cos_sin(to_turn(dot(x, pick_ref[...])))
        c_ref[...] = c
        s_ref[...] = s
        live = (start + lax.broadcasted_iota(jnp.int32, (size, 128), 0)) < fold_ref[patch]
        c0, c1, s0, s1 = c[:, :128], c[:, 128:], s[:, :128], s[:, 128:]
        real = jnp.where(live, c0 * c1 + s0 * s1, 0.0)
        imag = jnp.where(live, s0 * c1 - c0 * s1, 0.0)
        g_ref[:8, :] += jnp.sum(real.reshape(size // 8, 8, 128), axis=0)
        g_ref[8:, :] += jnp.sum(imag.reshape(size // 8, 8, 128), axis=0)

    whole = pl.BlockSpec((4, 8, 4096), lambda i: (0, 0, 0))
    return pl.pallas_call(
        body,
        grid=(SLOTS // size,),
        out_shape=(
            jax.ShapeDtypeStruct((SLOTS, 256), F32),
            jax.ShapeDtypeStruct((SLOTS, 256), F32),
            jax.ShapeDtypeStruct((16, 128), F32),
        ),
        in_specs=[
            pl.BlockSpec(memory_space=pltpu.SMEM),
            whole,
            whole,
            pl.BlockSpec((2, 8, 128), lambda i: (0, 0, 0)),
        ],
        out_specs=(
            pl.BlockSpec((size, 256), lambda i: (i, 0)),
            pl.BlockSpec((size, 256), lambda i: (i, 0)),
            pl.BlockSpec((16, 128), lambda i: (0, 0)),
        ),
        scratch_shapes=[pltpu.VMEM((16, 256), BF)],
        compiler_params=pltpu.CompilerParams(vmem_limit_bytes=VMEM),
        cost_estimate=pl.CostEstimate(flops=4 << 30, bytes_accessed=9 << 20, transcendentals=0),
        name="tables",
    )(fold, places, waves, chosen)


def pursue(received, cosine, sine, cross, fold, atoms):
    size, blocks, tall, ahead = 128, 8, 256, 3
    span = SLOTS // blocks
    parts = len(atoms)

    def body(fold_ref, g_ref, r_hbm, c_hbm, s_hbm, *rest):
        a_hbm, (o_ref, r_ref, c_ref, s_ref, a_ref, z_ref, sem, a_sem) = rest[:parts], rest[parts:]
        patch = lax.axis_index("xl") * 4 + lax.axis_index("z")
        loads = []
        for j in range(blocks):
            rows = pl.ds(j * span, span)
            loads.append(
                [
                    pltpu.make_async_copy(src.at[rows, :], dst.at[rows, :], sem.at[j, k])
                    for k, (src, dst) in enumerate([(r_hbm, r_ref), (c_hbm, c_ref), (s_hbm, s_ref)])
                ]
            )
        for j in range(3):
            for copy in loads[j]:
                copy.start()

        def stream(m):
            for k, (low, high) in enumerate([(0, EARLY), (EARLY, 2048)]):
                first, last = max(m * tall, low), min((m + 1) * tall, high)
                if first < last:
                    pltpu.make_async_copy(
                        a_hbm[k].at[pl.ds(first - low, last - first), :],
                        a_ref.at[pl.ds(first, last - first), :],
                        a_sem.at[m],
                    ).start()

        count = fold_ref[patch]
        inverse = 1.0 / jnp.full((1, 128), count, jnp.int32).astype(F32)
        zero = jnp.zeros((8, 128), F32)
        row = lax.broadcasted_iota(jnp.int32, (size, 128), 0)

        def fold8(v):
            return jnp.sum(v.reshape(size // 8, 8, 128), axis=0)

        def gather(j, sums):
            start = pl.multiple_of(j * size, size)
            rows = pl.ds(start, size)
            live = row < count - start
            c0, c1 = c_ref[rows, :128], c_ref[rows, 128:]
            s0, s1 = s_ref[rows, :128], s_ref[rows, 128:]
            re = jnp.where(live, r_ref[rows, :128].astype(F32), 0.0)
            im = jnp.where(live, r_ref[rows, 128:].astype(F32), 0.0)
            new = (re * c0 + im * s0, im * c0 - re * s0, re * c1 + im * s1, im * c1 - re * s1)
            return tuple(a + fold8(b) for a, b in zip(sums, new))

        sums = (zero,) * 4
        for j in range(blocks):
            for copy in loads[j]:
                copy.wait()
            if j + 3 < blocks:
                for copy in loads[j + 3]:
                    copy.start()
            elif j + 3 < blocks + ahead:
                stream(j + 3 - blocks)
            sums = lax.fori_loop(j * span // size, (j + 1) * span // size, gather, sums)
        r0, i0, r1, i1 = [jnp.sum(v, axis=0, keepdims=True) for v in sums]
        gr = jnp.sum(g_ref[:8, :], axis=0, keepdims=True)
        gi = jnp.sum(g_ref[8:, :], axis=0, keepdims=True)
        a0, b0 = r0 * inverse, i0 * inverse
        a1 = (r1 - (a0 * gr - b0 * gi)) * inverse
        b1 = (i1 - (a0 * gi + b0 * gr)) * inverse

        def split(v):
            first = v.astype(BF).astype(F32)
            second = (v - first).astype(BF).astype(F32)
            return [first, second, v - first - second]

        packed = [jnp.concatenate(pair, axis=1) for pair in zip(split(a0), split(b0))]
        packed += [jnp.concatenate(pair, axis=1) for pair in zip(split(a1), split(b1))]
        packed = jnp.concatenate(packed + [jnp.zeros((10, 256), F32)], axis=0).astype(BF)
        for b in range(8):
            o_ref[b, 256:, :] = packed

        def subtract(j, carry):
            start = pl.multiple_of(j * size, size)
            rows = pl.ds(start, size)
            live = row < count - start
            c0, c1 = c_ref[rows, :128], c_ref[rows, 128:]
            s0, s1 = s_ref[rows, :128], s_ref[rows, 128:]
            re = r_ref[rows, :128].astype(F32) - (a0 * c0 - b0 * s0) - (a1 * c1 - b1 * s1)
            im = r_ref[rows, 128:].astype(F32) - (a0 * s0 + b0 * c0) - (a1 * s1 + b1 * c1)
            re = jnp.where(live, re, 0.0).astype(BF)
            im = jnp.where(live, im, 0.0).astype(BF)
            z_ref[0, rows, :128] = re
            z_ref[0, rows, 128:] = im
            z_ref[1, rows, :128] = im
            z_ref[1, rows, 128:] = -re
            return carry

        lax.fori_loop(0, SLOTS // size, subtract, 0)

        def project(m, carry):
            rows = pl.ds(pl.multiple_of(m * tall, tall), tall)
            pltpu.make_async_copy(a_ref.at[rows, :], a_ref.at[rows, :], a_sem.at[m]).wait()
            for later in range(ahead, 2048 // tall):

                @pl.when(m == later - ahead)
                def _(later=later):
                    stream(later)

            acc = dot(a_ref[rows, :SLOTS], z_ref[0]) + dot(a_ref[rows, SLOTS:], z_ref[1])
            o_ref[m, :256, :] = acc.astype(BF)
            return carry

        lax.fori_loop(0, 2048 // tall, project, 0)

    hbm = pl.BlockSpec(memory_space=pl.ANY)
    whole = pl.BlockSpec(memory_space=pltpu.VMEM)
    return pl.pallas_call(
        body,
        out_shape=jax.ShapeDtypeStruct((8, 272, 256), BF),
        in_specs=[pl.BlockSpec(memory_space=pltpu.SMEM), whole] + [hbm] * (3 + parts),
        out_specs=whole,
        scratch_shapes=[
            pltpu.VMEM((SLOTS, 256), BF),
            pltpu.VMEM((SLOTS, 256), F32),
            pltpu.VMEM((SLOTS, 256), F32),
            pltpu.VMEM((2048, 2 * SLOTS), BF),
            pltpu.VMEM((2, SLOTS, 256), BF),
            pltpu.SemaphoreType.DMA((blocks, 3)),
            pltpu.SemaphoreType.DMA((2048 // tall,)),
        ],
        compiler_params=pltpu.CompilerParams(vmem_limit_bytes=VMEM),
        cost_estimate=pl.CostEstimate(flops=9 << 30, bytes_accessed=45 << 20, transcendentals=0),
        name="pursue",
    )(fold, cross, received, cosine, sine, *atoms)


def finish(moved):
    step = 128

    def body(a_ref, e_ref, o_ref, c_ref):
        for part in range(2):
            turned = jnp.swapaxes(a_ref[:, :, part * 128 : (part + 1) * 128].astype(F32), 0, 1)
            for k in range(step):
                o_ref[pl.ds(16 * k + part, 8, stride=2), :] = turned[k]

        @pl.when(pl.program_id(0) == 0)
        def _():
            for p in range(8):
                v = e_ref[p].astype(F32)
                for t in range(2):
                    total = v[3 * t : 3 * t + 1] + (v[3 * t + 1 : 3 * t + 2] + v[3 * t + 2 : 3 * t + 3])
                    row = t * 16 + 2 * p
                    c_ref[row : row + 1, :] = total[:, :128]
                    c_ref[row + 1 : row + 2, :] = total[:, 128:]

    return pl.pallas_call(
        body,
        grid=(256 // step,),
        out_shape=(jax.ShapeDtypeStruct((4096, 128), F32), jax.ShapeDtypeStruct((32, 128), F32)),
        in_specs=[
            pl.BlockSpec((8, step, 256), lambda i: (0, i, 0)),
            pl.BlockSpec((8, 16, 256), lambda i: (0, 16, 0)),
        ],
        out_specs=(
            pl.BlockSpec((step * 16, 128), lambda i: (i, 0)),
            pl.BlockSpec((32, 128), lambda i: (0, 0)),
        ),
        compiler_params=pltpu.CompilerParams(vmem_limit_bytes=VMEM),
        cost_estimate=pl.CostEstimate(flops=1 << 20, bytes_accessed=3 << 20, transcendentals=0),
        name="finish",
    )(moved, moved)


def local(traces, coords, wavenumbers, fold, selected):
    sent = dft(traces[0])
    moved = lax.all_to_all(sent, "freq", split_axis=0, concat_axis=0, tiled=True)
    both = jnp.concatenate([moved, moved], axis=0)
    moved = lax.all_to_all(both, TRACE, split_axis=0, concat_axis=0, tiled=True)
    early = make_atoms(wavenumbers, coords, 0, EARLY)
    late = make_atoms(wavenumbers, coords, EARLY, 2048 - EARLY)
    cosine, sine, cross = chosen_tables(coords, wavenumbers, selected, fold)
    sent = pursue(moved.reshape(SLOTS, 256), cosine, sine, cross, fold, [early, late])
    moved = lax.all_to_all(sent, EIGHT, split_axis=0, concat_axis=0, tiled=True)
    spectrum, coefficients = finish(moved)
    return spectrum.reshape(256, 8, 2, 128), coefficients.reshape(2, 8, 2, 128)


def solution(mesh):
    split = Mesh(mesh.devices.reshape(8, 2, 2, 4), ("freq",) + TRACE)
    return jax.shard_map(
        local,
        mesh=split,
        in_specs=(P("freq", TRACE, None), P(), P(), P(), P(None, None, "freq")),
        out_specs=(P(TRACE, None, None, "freq"), P(None, None, None, "freq")),
        check_vma=False,
    )
```

```python
import math

import jax
import jax.numpy as jnp
from jax import lax
from jax.experimental import pallas as pl
from jax.experimental.pallas import tpu as pltpu
from jax.sharding import Mesh
from jax.sharding import PartitionSpec as P


BF = jnp.bfloat16
F32 = jnp.float32
NT = 4096
SLOTS = 4096
TRACE = ("half", "xl", "z")
EIGHT = ("xl", "z")
ROUND = 12582912.0
R2 = math.sqrt(2.0)
VMEM = 62 << 20
EARLY = 896


def dot(a, b):
    return jnp.dot(a, b, preferred_element_type=F32)


def to_turn(t):
    return t - ((t + ROUND) - ROUND)


def cos_sin(r):
    y = r * r
    s = r * (
        R2 * 3.14159258
        + y * (R2 * -5.16770688 + y * (R2 * 2.55003138 + y * (R2 * -0.59804517 + y * (R2 * 0.07722012))))
    )
    c = R2 * 0.99999995 + y * (
        R2 * -4.93479286 + y * (R2 * 4.05841192 + y * (R2 * -1.33188016 + y * (R2 * 0.2196968)))
    )
    return 1.0 - s * s, s * c


def cos_sin_short(r):
    y = r * r
    s = r * (R2 * 3.14064003 + y * (R2 * -5.13690521 + y * (R2 * 2.29954682)))
    c = R2 * 0.9999933 + y * (R2 * -4.93393802 + y * (R2 * 4.04128385 + y * (R2 * -1.22212706)))
    return c * c - 1.0, s * c


def low_high(v):
    high = v >> 5
    return (v & 31).astype(F32), high.astype(F32)


def wave_rows(w):
    low, high = low_high(w)
    return jnp.concatenate([high * (1 / 32), low * (1 / 32), low * (1 / 1024), jnp.zeros_like(low)], axis=0)


def place_rows(x):
    low, high = low_high(x)
    return jnp.concatenate([low, high, low, jnp.zeros_like(low)], axis=0)


def patch_rows(ref, patch, start, size):
    return jnp.concatenate([ref[c, pl.ds(patch, 1), pl.ds(start, size)] for c in range(4)], axis=0)


def dft(traces):
    half = NT // 2
    width = 256

    def body(x_ref, o_ref):
        f = pl.program_id(0) * width + lax.broadcasted_iota(jnp.int32, (64, width), 1)
        n = lax.broadcasted_iota(jnp.int32, (64, width), 0)

        def table(step):
            m = (n * f * step) & (NT - 1)
            m = jnp.where(m >= half, m - NT, m)
            return cos_sin(m.astype(F32) * (1.0 / NT))

        c_far, s_far = table(64)
        c_near, s_near = table(1)
        acc = jnp.zeros((512, 2 * width), F32)
        for chunk in range(half // 256):
            rows = []
            for a in range(chunk * 4, chunk * 4 + 4):
                ca, sa = c_far[a : a + 1, :], s_far[a : a + 1, :]
                real = (ca * c_near - sa * s_near).astype(BF)
                imag = (-(sa * c_near) - ca * s_near).astype(BF)
                rows.append(jnp.concatenate([real, imag], axis=1))
            low = x_ref[:, chunk * 256 : (chunk + 1) * 256]
            high = x_ref[:, half + chunk * 256 : half + (chunk + 1) * 256]
            acc = acc + dot(jnp.concatenate([low, high], axis=0), jnp.concatenate(rows, axis=0))
        odd = (lax.broadcasted_iota(jnp.int32, (256, 2 * width), 1) & 1) == 1
        both = jnp.where(odd, acc[:256] - acc[256:], acc[:256] + acc[256:]).astype(BF)
        for g in range(width // 128):
            lanes = slice(g * 128, (g + 1) * 128)
            o_ref[g, :, :128] = both[:, :width][:, lanes]
            o_ref[g, :, 128:] = both[:, width:][:, lanes]

    return pl.pallas_call(
        body,
        grid=(1024 // width,),
        out_shape=jax.ShapeDtypeStruct((8, 256, 256), BF),
        in_specs=[pl.BlockSpec((256, NT), lambda i: (0, 0))],
        out_specs=pl.BlockSpec((width // 128, 256, 256), lambda i: (i, 0, 0)),
        compiler_params=pltpu.CompilerParams(vmem_limit_bytes=VMEM),
        cost_estimate=pl.CostEstimate(flops=2 * 256 * NT * 2048, bytes_accessed=3 << 20, transcendentals=0),
        name="dft",
    )(traces)


def make_atoms(waves, places, first, count):
    rows = 128

    def body(w_ref, x_ref, o_ref, place_ref, wave_ref):
        patch = lax.axis_index("xl") * 4 + lax.axis_index("z")

        @pl.when(pl.program_id(0) == 0)
        def _():
            place_ref[...] = place_rows(patch_rows(x_ref, patch, 0, SLOTS)).astype(BF)
            wave_ref[...] = wave_rows(patch_rows(w_ref, patch, 0, 4096))

        start = lax.axis_index("half") * 2048 + first + pl.program_id(0) * rows
        start = pl.multiple_of(start, rows)
        w = jnp.transpose(wave_ref[:, pl.ds(start, rows)]).astype(BF)
        for j in range(16):
            c, s = cos_sin_short(to_turn(dot(w, place_ref[:, j * 256 : (j + 1) * 256])))
            o_ref[:, j * 256 : (j + 1) * 256] = c.astype(BF)
            o_ref[:, SLOTS + j * 256 : SLOTS + (j + 1) * 256] = s.astype(BF)

    whole = pl.BlockSpec((4, 8, 4096), lambda i: (0, 0, 0))
    return pl.pallas_call(
        body,
        grid=(count // rows,),
        out_shape=jax.ShapeDtypeStruct((count, 2 * SLOTS), BF),
        in_specs=[whole, whole],
        out_specs=pl.BlockSpec((rows, 2 * SLOTS), lambda i: (i, 0)),
        scratch_shapes=[pltpu.VMEM((16, SLOTS), BF), pltpu.VMEM((16, 4096), F32)],
        compiler_params=pltpu.CompilerParams(vmem_limit_bytes=VMEM),
        cost_estimate=pl.CostEstimate(flops=count * (15 << 20), bytes_accessed=count * 16384, transcendentals=0),
        name="atoms",
    )(waves, places)


def chosen_tables(places, waves, chosen, fold):
    size = 512

    def body(fold_ref, x_ref, w_ref, ch_ref, c_ref, s_ref, g_ref, pick_ref):
        patch = lax.axis_index("xl") * 4 + lax.axis_index("z")
        step = pl.program_id(0)

        @pl.when(step == 0)
        def _():
            rows = [w_ref[c, pl.ds(patch, 1), :] for c in range(4)]
            table3 = rows[0] + rows[1] * 1024 + rows[2] * (1 << 20)
            index = jnp.concatenate([ch_ref[t, pl.ds(patch, 1), :] for t in range(2)] * 4, axis=0)
            low, high = index & 127, index >> 7
            found3 = jnp.zeros((8, 128), jnp.int32)
            found1 = jnp.zeros((8, 128), jnp.int32)
            for r in range(32):
                here = high == r
                lanes = slice(r * 128, (r + 1) * 128)
                g3 = jnp.take_along_axis(jnp.broadcast_to(table3[:, lanes], (8, 128)), low, axis=1)
                g1 = jnp.take_along_axis(jnp.broadcast_to(rows[3][:, lanes], (8, 128)), low, axis=1)
                found3 = jnp.where(here, g3, found3)
                found1 = jnp.where(here, g1, found1)
            parts = [found3 & 1023, (found3 >> 10) & 1023, found3 >> 20, found1]
            picked = [jnp.concatenate([v[t : t + 1] for v in parts], axis=0) for t in range(2)]
            pick_ref[...] = wave_rows(jnp.concatenate(picked, axis=1)).astype(BF)
            g_ref[...] = jnp.zeros((16, 128), F32)

        start = pl.multiple_of(step * size, size)
        x = jnp.transpose(place_rows(patch_rows(x_ref, patch, start, size))).astype(BF)
        c, s = cos_sin(to_turn(dot(x, pick_ref[...])))
        c_ref[...] = c
        s_ref[...] = s
        live = (start + lax.broadcasted_iota(jnp.int32, (size, 128), 0)) < fold_ref[patch]
        c0, c1, s0, s1 = c[:, :128], c[:, 128:], s[:, :128], s[:, 128:]
        real = jnp.where(live, c0 * c1 + s0 * s1, 0.0)
        imag = jnp.where(live, s0 * c1 - c0 * s1, 0.0)
        g_ref[:8, :] += jnp.sum(real.reshape(size // 8, 8, 128), axis=0)
        g_ref[8:, :] += jnp.sum(imag.reshape(size // 8, 8, 128), axis=0)

    whole = pl.BlockSpec((4, 8, 4096), lambda i: (0, 0, 0))
    return pl.pallas_call(
        body,
        grid=(SLOTS // size,),
        out_shape=(
            jax.ShapeDtypeStruct((SLOTS, 256), F32),
            jax.ShapeDtypeStruct((SLOTS, 256), F32),
            jax.ShapeDtypeStruct((16, 128), F32),
        ),
        in_specs=[
            pl.BlockSpec(memory_space=pltpu.SMEM),
            whole,
            whole,
            pl.BlockSpec((2, 8, 128), lambda i: (0, 0, 0)),
        ],
        out_specs=(
            pl.BlockSpec((size, 256), lambda i: (i, 0)),
            pl.BlockSpec((size, 256), lambda i: (i, 0)),
            pl.BlockSpec((16, 128), lambda i: (0, 0)),
        ),
        scratch_shapes=[pltpu.VMEM((16, 256), BF)],
        compiler_params=pltpu.CompilerParams(vmem_limit_bytes=VMEM),
        cost_estimate=pl.CostEstimate(flops=4 << 30, bytes_accessed=9 << 20, transcendentals=0),
        name="tables",
    )(fold, places, waves, chosen)


def pursue(received, cosine, sine, cross, fold, atoms):
    size, blocks, tall, ahead = 128, 8, 256, 3
    span = SLOTS // blocks
    parts = len(atoms)

    def body(fold_ref, g_ref, r_hbm, c_hbm, s_hbm, *rest):
        a_hbm, (o_ref, r_ref, c_ref, s_ref, a_ref, z_ref, sem, a_sem) = rest[:parts], rest[parts:]
        patch = lax.axis_index("xl") * 4 + lax.axis_index("z")
        loads = []
        for j in range(blocks):
            rows = pl.ds(j * span, span)
            loads.append(
                [
                    pltpu.make_async_copy(src.at[rows, :], dst.at[rows, :], sem.at[j, k])
                    for k, (src, dst) in enumerate([(r_hbm, r_ref), (c_hbm, c_ref), (s_hbm, s_ref)])
                ]
            )
        for j in range(3):
            for copy in loads[j]:
                copy.start()

        def stream(m):
            for k, (low, high) in enumerate([(0, EARLY), (EARLY, 2048)]):
                first, last = max(m * tall, low), min((m + 1) * tall, high)
                if first < last:
                    pltpu.make_async_copy(
                        a_hbm[k].at[pl.ds(first - low, last - first), :],
                        a_ref.at[pl.ds(first, last - first), :],
                        a_sem.at[m],
                    ).start()

        count = fold_ref[patch]
        inverse = 1.0 / jnp.full((1, 128), count, jnp.int32).astype(F32)
        zero = jnp.zeros((8, 128), F32)
        row = lax.broadcasted_iota(jnp.int32, (size, 128), 0)

        def fold8(v):
            return jnp.sum(v.reshape(size // 8, 8, 128), axis=0)

        def gather(j, sums):
            start = pl.multiple_of(j * size, size)
            rows = pl.ds(start, size)
            live = row < count - start
            c0, c1 = c_ref[rows, :128], c_ref[rows, 128:]
            s0, s1 = s_ref[rows, :128], s_ref[rows, 128:]
            re = jnp.where(live, r_ref[rows, :128].astype(F32), 0.0)
            im = jnp.where(live, r_ref[rows, 128:].astype(F32), 0.0)
            new = (re * c0 + im * s0, im * c0 - re * s0, re * c1 + im * s1, im * c1 - re * s1)
            return tuple(a + fold8(b) for a, b in zip(sums, new))

        sums = (zero,) * 4
        for j in range(blocks):
            for copy in loads[j]:
                copy.wait()
            if j + 3 < blocks:
                for copy in loads[j + 3]:
                    copy.start()
            elif j + 3 < blocks + ahead:
                stream(j + 3 - blocks)
            sums = lax.fori_loop(j * span // size, (j + 1) * span // size, gather, sums)
        r0, i0, r1, i1 = [jnp.sum(v, axis=0, keepdims=True) for v in sums]
        gr = jnp.sum(g_ref[:8, :], axis=0, keepdims=True)
        gi = jnp.sum(g_ref[8:, :], axis=0, keepdims=True)
        a0, b0 = r0 * inverse, i0 * inverse
        a1 = (r1 - (a0 * gr - b0 * gi)) * inverse
        b1 = (i1 - (a0 * gi + b0 * gr)) * inverse

        def split(v):
            first = v.astype(BF).astype(F32)
            second = (v - first).astype(BF).astype(F32)
            return [first, second, v - first - second]

        packed = [jnp.concatenate(pair, axis=1) for pair in zip(split(a0), split(b0))]
        packed += [jnp.concatenate(pair, axis=1) for pair in zip(split(a1), split(b1))]
        packed = jnp.concatenate(packed + [jnp.zeros((2, 256), F32)], axis=0).astype(BF)
        for b in range(8):
            o_ref[b, 256:, :] = packed

        def subtract(j, carry):
            start = pl.multiple_of(j * size, size)
            rows = pl.ds(start, size)
            live = row < count - start
            c0, c1 = c_ref[rows, :128], c_ref[rows, 128:]
            s0, s1 = s_ref[rows, :128], s_ref[rows, 128:]
            re = r_ref[rows, :128].astype(F32) - (a0 * c0 - b0 * s0) - (a1 * c1 - b1 * s1)
            im = r_ref[rows, 128:].astype(F32) - (a0 * s0 + b0 * c0) - (a1 * s1 + b1 * c1)
            re = jnp.where(live, re, 0.0).astype(BF)
            im = jnp.where(live, im, 0.0).astype(BF)
            z_ref[0, rows, :128] = re
            z_ref[0, rows, 128:] = im
            z_ref[1, rows, :128] = im
            z_ref[1, rows, 128:] = -re
            return carry

        lax.fori_loop(0, SLOTS // size, subtract, 0)

        def project(m, carry):
            rows = pl.ds(pl.multiple_of(m * tall, tall), tall)
            pltpu.make_async_copy(a_ref.at[rows, :], a_ref.at[rows, :], a_sem.at[m]).wait()
            for later in range(ahead, 2048 // tall):

                @pl.when(m == later - ahead)
                def _(later=later):
                    stream(later)

            acc = dot(a_ref[rows, :SLOTS], z_ref[0]) + dot(a_ref[rows, SLOTS:], z_ref[1])
            o_ref[m, :256, :] = acc.astype(BF)
            return carry

        lax.fori_loop(0, 2048 // tall, project, 0)

    hbm = pl.BlockSpec(memory_space=pl.ANY)
    whole = pl.BlockSpec(memory_space=pltpu.VMEM)
    return pl.pallas_call(
        body,
        out_shape=jax.ShapeDtypeStruct((8, 264, 256), BF),
        in_specs=[pl.BlockSpec(memory_space=pltpu.SMEM), whole] + [hbm] * (3 + parts),
        out_specs=whole,
        scratch_shapes=[
            pltpu.VMEM((SLOTS, 256), BF),
            pltpu.VMEM((SLOTS, 256), F32),
            pltpu.VMEM((SLOTS, 256), F32),
            pltpu.VMEM((2048, 2 * SLOTS), BF),
            pltpu.VMEM((2, SLOTS, 256), BF),
            pltpu.SemaphoreType.DMA((blocks, 3)),
            pltpu.SemaphoreType.DMA((2048 // tall,)),
        ],
        compiler_params=pltpu.CompilerParams(vmem_limit_bytes=50 << 20),
        cost_estimate=pl.CostEstimate(flops=9 << 30, bytes_accessed=45 << 20, transcendentals=0),
        name="pursue",
    )(fold, cross, received, cosine, sine, *atoms)


def finish(moved):
    step = 128

    def body(a_ref, e_ref, o_ref, c_ref):
        for part in range(2):
            turned = jnp.swapaxes(a_ref[:, :, part * 128 : (part + 1) * 128].astype(F32), 0, 1)
            for k in range(step):
                o_ref[pl.ds(16 * k + part, 8, stride=2), :] = turned[k]

        @pl.when(pl.program_id(0) == 0)
        def _():
            for p in range(8):
                v = e_ref[p].astype(F32)
                for t in range(2):
                    total = v[3 * t : 3 * t + 1] + (v[3 * t + 1 : 3 * t + 2] + v[3 * t + 2 : 3 * t + 3])
                    row = t * 16 + 2 * p
                    c_ref[row : row + 1, :] = total[:, :128]
                    c_ref[row + 1 : row + 2, :] = total[:, 128:]

    return pl.pallas_call(
        body,
        grid=(256 // step,),
        out_shape=(jax.ShapeDtypeStruct((4096, 128), F32), jax.ShapeDtypeStruct((32, 128), F32)),
        in_specs=[
            pl.BlockSpec((8, step, 256), lambda i: (0, i, 0)),
            pl.BlockSpec((8, 8, 256), lambda i: (0, 32, 0)),
        ],
        out_specs=(
            pl.BlockSpec((step * 16, 128), lambda i: (i, 0)),
            pl.BlockSpec((32, 128), lambda i: (0, 0)),
        ),
        compiler_params=pltpu.CompilerParams(vmem_limit_bytes=16 << 20),
        cost_estimate=pl.CostEstimate(flops=1 << 20, bytes_accessed=3 << 20, transcendentals=0),
        name="finish",
    )(moved, moved)


def local(traces, coords, wavenumbers, fold, selected):
    sent = dft(traces[0])
    moved = lax.all_to_all(sent, "freq", split_axis=0, concat_axis=0, tiled=True)
    both = jnp.concatenate([moved, moved], axis=0)
    moved = lax.all_to_all(both, TRACE, split_axis=0, concat_axis=0, tiled=True)
    early = make_atoms(wavenumbers, coords, 0, EARLY)
    late = make_atoms(wavenumbers, coords, EARLY, 2048 - EARLY)
    cosine, sine, cross = chosen_tables(coords, wavenumbers, selected, fold)
    sent = pursue(moved.reshape(SLOTS, 256), cosine, sine, cross, fold, [early, late])
    moved = lax.all_to_all(sent, EIGHT, split_axis=0, concat_axis=0, tiled=True)
    spectrum, coefficients = finish(moved)
    return spectrum.reshape(256, 8, 2, 128), coefficients.reshape(2, 8, 2, 128)


def solution(mesh):
    split = Mesh(mesh.devices.reshape(8, 2, 2, 4), ("freq",) + TRACE)
    return jax.shard_map(
        local,
        mesh=split,
        in_specs=(P("freq", TRACE, None), P(), P(), P(), P(None, None, "freq")),
        out_specs=(P(TRACE, None, None, "freq"), P(None, None, None, "freq")),
        check_vma=False,
    )
```

```python
import math

import jax
import jax.numpy as jnp
from jax import lax
from jax.experimental import pallas as pl
from jax.experimental.pallas import tpu as pltpu
from jax.sharding import Mesh
from jax.sharding import PartitionSpec as P


BF = jnp.bfloat16
F32 = jnp.float32
NT = 4096
SLOTS = 4096
TRACE = ("half", "xl", "z")
EIGHT = ("xl", "z")
ROUND = 12582912.0
R2 = math.sqrt(2.0)
VMEM = 62 << 20
EARLY = 896


def dot(a, b):
    return jnp.dot(a, b, preferred_element_type=F32)


def to_turn(t):
    return t - ((t + ROUND) - ROUND)


def cos_sin(r):
    y = r * r
    s = r * (
        R2 * 3.14159258
        + y * (R2 * -5.16770688 + y * (R2 * 2.55003138 + y * (R2 * -0.59804517 + y * (R2 * 0.07722012))))
    )
    c = R2 * 0.99999995 + y * (
        R2 * -4.93479286 + y * (R2 * 4.05841192 + y * (R2 * -1.33188016 + y * (R2 * 0.2196968)))
    )
    return 1.0 - s * s, s * c


def cos_sin_short(r):
    y = r * r
    s = r * (R2 * 3.14064003 + y * (R2 * -5.13690521 + y * (R2 * 2.29954682)))
    c = R2 * 0.9999933 + y * (R2 * -4.93393802 + y * (R2 * 4.04128385 + y * (R2 * -1.22212706)))
    return c * c - 1.0, s * c


def low_high(v):
    high = v >> 5
    return (v & 31).astype(F32), high.astype(F32)


def wave_rows(w):
    low, high = low_high(w)
    return jnp.concatenate([high * (1 / 32), low * (1 / 32), low * (1 / 1024), jnp.zeros_like(low)], axis=0)


def place_rows(x):
    low, high = low_high(x)
    return jnp.concatenate([low, high, low, jnp.zeros_like(low)], axis=0)


def patch_rows(ref, patch, start, size):
    return jnp.concatenate([ref[c, pl.ds(patch, 1), pl.ds(start, size)] for c in range(4)], axis=0)


def dft(traces):
    half = NT // 2
    width = 256

    def body(x_ref, o_ref):
        f = pl.program_id(0) * width + lax.broadcasted_iota(jnp.int32, (64, width), 1)
        n = lax.broadcasted_iota(jnp.int32, (64, width), 0)

        def table(step):
            m = (n * f * step) & (NT - 1)
            m = jnp.where(m >= half, m - NT, m)
            return cos_sin(m.astype(F32) * (1.0 / NT))

        c_far, s_far = table(64)
        c_near, s_near = table(1)
        acc = jnp.zeros((512, 2 * width), F32)
        for chunk in range(half // 256):
            rows = []
            for a in range(chunk * 4, chunk * 4 + 4):
                ca, sa = c_far[a : a + 1, :], s_far[a : a + 1, :]
                real = (ca * c_near - sa * s_near).astype(BF)
                imag = (-(sa * c_near) - ca * s_near).astype(BF)
                rows.append(jnp.concatenate([real, imag], axis=1))
            low = x_ref[:, chunk * 256 : (chunk + 1) * 256]
            high = x_ref[:, half + chunk * 256 : half + (chunk + 1) * 256]
            acc = acc + dot(jnp.concatenate([low, high], axis=0), jnp.concatenate(rows, axis=0))
        odd = (lax.broadcasted_iota(jnp.int32, (256, 2 * width), 1) & 1) == 1
        both = jnp.where(odd, acc[:256] - acc[256:], acc[:256] + acc[256:]).astype(BF)
        for g in range(width // 128):
            lanes = slice(g * 128, (g + 1) * 128)
            o_ref[g, :, :128] = both[:, :width][:, lanes]
            o_ref[g, :, 128:] = both[:, width:][:, lanes]

    return pl.pallas_call(
        body,
        grid=(1024 // width,),
        out_shape=jax.ShapeDtypeStruct((8, 256, 256), BF),
        in_specs=[pl.BlockSpec((256, NT), lambda i: (0, 0))],
        out_specs=pl.BlockSpec((width // 128, 256, 256), lambda i: (i, 0, 0)),
        compiler_params=pltpu.CompilerParams(vmem_limit_bytes=VMEM),
        cost_estimate=pl.CostEstimate(flops=2 * 256 * NT * 2048, bytes_accessed=3 << 20, transcendentals=0),
        name="dft",
    )(traces)


def twice(blocks):
    def body(x_ref, o_ref, sem):
        copies = [pltpu.make_async_copy(x_ref, o_ref.at[pl.ds(8 * k, 8)], sem.at[k]) for k in range(2)]
        for copy in copies:
            copy.start()
        for copy in copies:
            copy.wait()

    return pl.pallas_call(
        body,
        out_shape=jax.ShapeDtypeStruct((16, 256, 256), BF),
        in_specs=[pl.BlockSpec(memory_space=pltpu.VMEM)],
        out_specs=pl.BlockSpec(memory_space=pl.ANY),
        scratch_shapes=[pltpu.SemaphoreType.DMA((2,))],
        compiler_params=pltpu.CompilerParams(vmem_limit_bytes=8 << 20),
        cost_estimate=pl.CostEstimate(flops=1 << 20, bytes_accessed=3 << 20, transcendentals=0),
        name="twice",
    )(blocks)


def make_atoms(waves, places, first, count):
    rows = 128

    def body(w_ref, x_ref, o_ref, place_ref, wave_ref):
        patch = lax.axis_index("xl") * 4 + lax.axis_index("z")

        @pl.when(pl.program_id(0) == 0)
        def _():
            place_ref[...] = place_rows(patch_rows(x_ref, patch, 0, SLOTS)).astype(BF)
            wave_ref[...] = wave_rows(patch_rows(w_ref, patch, 0, 4096))

        start = lax.axis_index("half") * 2048 + first + pl.program_id(0) * rows
        start = pl.multiple_of(start, rows)
        w = jnp.transpose(wave_ref[:, pl.ds(start, rows)]).astype(BF)
        for j in range(16):
            c, s = cos_sin_short(to_turn(dot(w, place_ref[:, j * 256 : (j + 1) * 256])))
            o_ref[:, j * 256 : (j + 1) * 256] = c.astype(BF)
            o_ref[:, SLOTS + j * 256 : SLOTS + (j + 1) * 256] = s.astype(BF)

    whole = pl.BlockSpec((4, 8, 4096), lambda i: (0, 0, 0))
    return pl.pallas_call(
        body,
        grid=(count // rows,),
        out_shape=jax.ShapeDtypeStruct((count, 2 * SLOTS), BF),
        in_specs=[whole, whole],
        out_specs=pl.BlockSpec((rows, 2 * SLOTS), lambda i: (i, 0)),
        scratch_shapes=[pltpu.VMEM((16, SLOTS), BF), pltpu.VMEM((16, 4096), F32)],
        compiler_params=pltpu.CompilerParams(vmem_limit_bytes=VMEM),
        cost_estimate=pl.CostEstimate(flops=count * (15 << 20), bytes_accessed=count * 16384, transcendentals=0),
        name="atoms",
    )(waves, places)


def chosen_tables(places, waves, chosen, fold):
    size = 512

    def body(fold_ref, x_ref, w_ref, ch_ref, c_ref, s_ref, g_ref, pick_ref):
        patch = lax.axis_index("xl") * 4 + lax.axis_index("z")
        step = pl.program_id(0)

        @pl.when(step == 0)
        def _():
            rows = [w_ref[c, pl.ds(patch, 1), :] for c in range(4)]
            table3 = rows[0] + rows[1] * 1024 + rows[2] * (1 << 20)
            index = jnp.concatenate([ch_ref[t, pl.ds(patch, 1), :] for t in range(2)] * 4, axis=0)
            low, high = index & 127, index >> 7
            found3 = jnp.zeros((8, 128), jnp.int32)
            found1 = jnp.zeros((8, 128), jnp.int32)
            for r in range(32):
                here = high == r
                lanes = slice(r * 128, (r + 1) * 128)
                g3 = jnp.take_along_axis(jnp.broadcast_to(table3[:, lanes], (8, 128)), low, axis=1)
                g1 = jnp.take_along_axis(jnp.broadcast_to(rows[3][:, lanes], (8, 128)), low, axis=1)
                found3 = jnp.where(here, g3, found3)
                found1 = jnp.where(here, g1, found1)
            parts = [found3 & 1023, (found3 >> 10) & 1023, found3 >> 20, found1]
            picked = [jnp.concatenate([v[t : t + 1] for v in parts], axis=0) for t in range(2)]
            pick_ref[...] = wave_rows(jnp.concatenate(picked, axis=1)).astype(BF)
            g_ref[...] = jnp.zeros((16, 128), F32)

        start = pl.multiple_of(step * size, size)
        x = jnp.transpose(place_rows(patch_rows(x_ref, patch, start, size))).astype(BF)
        c, s = cos_sin(to_turn(dot(x, pick_ref[...])))
        c_ref[...] = c
        s_ref[...] = s
        live = (start + lax.broadcasted_iota(jnp.int32, (size, 128), 0)) < fold_ref[patch]
        c0, c1, s0, s1 = c[:, :128], c[:, 128:], s[:, :128], s[:, 128:]
        real = jnp.where(live, c0 * c1 + s0 * s1, 0.0)
        imag = jnp.where(live, s0 * c1 - c0 * s1, 0.0)
        g_ref[:8, :] += jnp.sum(real.reshape(size // 8, 8, 128), axis=0)
        g_ref[8:, :] += jnp.sum(imag.reshape(size // 8, 8, 128), axis=0)

    whole = pl.BlockSpec((4, 8, 4096), lambda i: (0, 0, 0))
    return pl.pallas_call(
        body,
        grid=(SLOTS // size,),
        out_shape=(
            jax.ShapeDtypeStruct((SLOTS, 256), F32),
            jax.ShapeDtypeStruct((SLOTS, 256), F32),
            jax.ShapeDtypeStruct((16, 1 << 17), F32),
        ),
        in_specs=[
            pl.BlockSpec(memory_space=pltpu.SMEM),
            whole,
            whole,
            pl.BlockSpec((2, 8, 128), lambda i: (0, 0, 0)),
        ],
        out_specs=(
            pl.BlockSpec((size, 256), lambda i: (i, 0)),
            pl.BlockSpec((size, 256), lambda i: (i, 0)),
            pl.BlockSpec((16, 128), lambda i: (0, 0)),
        ),
        scratch_shapes=[pltpu.VMEM((16, 256), BF)],
        compiler_params=pltpu.CompilerParams(vmem_limit_bytes=VMEM),
        cost_estimate=pl.CostEstimate(flops=4 << 30, bytes_accessed=9 << 20, transcendentals=0),
        name="tables",
    )(fold, places, waves, chosen)


def pursue(received, cosine, sine, cross, fold, atoms):
    size, blocks, tall, ahead = 128, 8, 256, 3
    span = SLOTS // blocks
    parts = len(atoms)

    def body(fold_ref, g_hbm, r_hbm, c_hbm, s_hbm, *rest):
        a_hbm, (o_ref, g_ref, r_ref, c_ref, s_ref, a_ref, z_ref, g_sem, sem, a_sem) = rest[:parts], rest[parts:]
        patch = lax.axis_index("xl") * 4 + lax.axis_index("z")
        cross_copy = pltpu.make_async_copy(g_hbm.at[:, :128], g_ref, g_sem)
        cross_copy.start()
        loads = []
        for j in range(blocks):
            rows = pl.ds(j * span, span)
            loads.append(
                [
                    pltpu.make_async_copy(src.at[rows, :], dst.at[rows, :], sem.at[j, k])
                    for k, (src, dst) in enumerate([(r_hbm, r_ref), (c_hbm, c_ref), (s_hbm, s_ref)])
                ]
            )
        for j in range(3):
            for copy in loads[j]:
                copy.start()

        def stream(m):
            for k, (low, high) in enumerate([(0, EARLY), (EARLY, 2048)]):
                first, last = max(m * tall, low), min((m + 1) * tall, high)
                if first < last:
                    pltpu.make_async_copy(
                        a_hbm[k].at[pl.ds(first - low, last - first), :],
                        a_ref.at[pl.ds(first, last - first), :],
                        a_sem.at[m],
                    ).start()

        count = fold_ref[patch]
        inverse = 1.0 / jnp.full((1, 128), count, jnp.int32).astype(F32)
        zero = jnp.zeros((8, 128), F32)
        row = lax.broadcasted_iota(jnp.int32, (size, 128), 0)

        def fold8(v):
            return jnp.sum(v.reshape(size // 8, 8, 128), axis=0)

        def gather(j, sums):
            start = pl.multiple_of(j * size, size)
            rows = pl.ds(start, size)
            live = row < count - start
            c0, c1 = c_ref[rows, :128], c_ref[rows, 128:]
            s0, s1 = s_ref[rows, :128], s_ref[rows, 128:]
            re = jnp.where(live, r_ref[rows, :128].astype(F32), 0.0)
            im = jnp.where(live, r_ref[rows, 128:].astype(F32), 0.0)
            new = (re * c0 + im * s0, im * c0 - re * s0, re * c1 + im * s1, im * c1 - re * s1)
            return tuple(a + fold8(b) for a, b in zip(sums, new))

        sums = (zero,) * 4
        for j in range(blocks):
            for copy in loads[j]:
                copy.wait()
            if j + 3 < blocks:
                for copy in loads[j + 3]:
                    copy.start()
            elif j + 3 < blocks + ahead:
                stream(j + 3 - blocks)
            sums = lax.fori_loop(j * span // size, (j + 1) * span // size, gather, sums)
        r0, i0, r1, i1 = [jnp.sum(v, axis=0, keepdims=True) for v in sums]
        cross_copy.wait()
        gr = jnp.sum(g_ref[:8, :], axis=0, keepdims=True)
        gi = jnp.sum(g_ref[8:, :], axis=0, keepdims=True)
        a0, b0 = r0 * inverse, i0 * inverse
        a1 = (r1 - (a0 * gr - b0 * gi)) * inverse
        b1 = (i1 - (a0 * gi + b0 * gr)) * inverse

        def split(v):
            first = v.astype(BF).astype(F32)
            second = (v - first).astype(BF).astype(F32)
            return [first, second, v - first - second]

        packed = [jnp.concatenate(pair, axis=1) for pair in zip(split(a0), split(b0))]
        packed += [jnp.concatenate(pair, axis=1) for pair in zip(split(a1), split(b1))]
        packed = jnp.concatenate(packed + [jnp.zeros((2, 256), F32)], axis=0).astype(BF)
        for b in range(8):
            o_ref[b, 256:, :] = packed

        def subtract(j, carry):
            start = pl.multiple_of(j * size, size)
            rows = pl.ds(start, size)
            live = row < count - start
            c0, c1 = c_ref[rows, :128], c_ref[rows, 128:]
            s0, s1 = s_ref[rows, :128], s_ref[rows, 128:]
            re = r_ref[rows, :128].astype(F32) - (a0 * c0 - b0 * s0) - (a1 * c1 - b1 * s1)
            im = r_ref[rows, 128:].astype(F32) - (a0 * s0 + b0 * c0) - (a1 * s1 + b1 * c1)
            re = jnp.where(live, re, 0.0).astype(BF)
            im = jnp.where(live, im, 0.0).astype(BF)
            z_ref[0, rows, :128] = re
            z_ref[0, rows, 128:] = im
            z_ref[1, rows, :128] = im
            z_ref[1, rows, 128:] = -re
            return carry

        lax.fori_loop(0, SLOTS // size, subtract, 0)

        def project(m, carry):
            rows = pl.ds(pl.multiple_of(m * tall, tall), tall)
            pltpu.make_async_copy(a_ref.at[rows, :], a_ref.at[rows, :], a_sem.at[m]).wait()
            for later in range(ahead, 2048 // tall):

                @pl.when(m == later - ahead)
                def _(later=later):
                    stream(later)

            acc = dot(a_ref[rows, :SLOTS], z_ref[0]) + dot(a_ref[rows, SLOTS:], z_ref[1])
            o_ref[m, :256, :] = acc.astype(BF)
            return carry

        lax.fori_loop(0, 2048 // tall, project, 0)

    hbm = pl.BlockSpec(memory_space=pl.ANY)
    whole = pl.BlockSpec(memory_space=pltpu.VMEM)
    return pl.pallas_call(
        body,
        out_shape=jax.ShapeDtypeStruct((8, 264, 256), BF),
        in_specs=[pl.BlockSpec(memory_space=pltpu.SMEM)] + [hbm] * (4 + parts),
        out_specs=whole,
        scratch_shapes=[
            pltpu.VMEM((16, 128), F32),
            pltpu.VMEM((SLOTS, 256), BF),
            pltpu.VMEM((SLOTS, 256), F32),
            pltpu.VMEM((SLOTS, 256), F32),
            pltpu.VMEM((2048, 2 * SLOTS), BF),
            pltpu.VMEM((2, SLOTS, 256), BF),
            pltpu.SemaphoreType.DMA(()),
            pltpu.SemaphoreType.DMA((blocks, 3)),
            pltpu.SemaphoreType.DMA((2048 // tall,)),
        ],
        compiler_params=pltpu.CompilerParams(vmem_limit_bytes=52 << 20),
        cost_estimate=pl.CostEstimate(flops=9 << 30, bytes_accessed=45 << 20, transcendentals=0),
        name="pursue",
    )(fold, cross, received, cosine, sine, *atoms)


def finish(moved):
    step = 128

    def body(a_ref, e_ref, o_ref, c_ref):
        for part in range(2):
            turned = jnp.swapaxes(a_ref[:, :, part * 128 : (part + 1) * 128].astype(F32), 0, 1)
            for k in range(step):
                o_ref[pl.ds(16 * k + part, 8, stride=2), :] = turned[k]

        @pl.when(pl.program_id(0) == 0)
        def _():
            for p in range(8):
                v = e_ref[p].astype(F32)
                for t in range(2):
                    total = v[3 * t : 3 * t + 1] + (v[3 * t + 1 : 3 * t + 2] + v[3 * t + 2 : 3 * t + 3])
                    row = t * 16 + 2 * p
                    c_ref[row : row + 1, :] = total[:, :128]
                    c_ref[row + 1 : row + 2, :] = total[:, 128:]

    return pl.pallas_call(
        body,
        grid=(256 // step,),
        out_shape=(jax.ShapeDtypeStruct((4096, 128), F32), jax.ShapeDtypeStruct((32, 128), F32)),
        in_specs=[
            pl.BlockSpec((8, step, 256), lambda i: (0, i, 0)),
            pl.BlockSpec((8, 8, 256), lambda i: (0, 32, 0)),
        ],
        out_specs=(
            pl.BlockSpec((step * 16, 128), lambda i: (i, 0)),
            pl.BlockSpec((32, 128), lambda i: (0, 0)),
        ),
        compiler_params=pltpu.CompilerParams(vmem_limit_bytes=16 << 20),
        cost_estimate=pl.CostEstimate(flops=1 << 20, bytes_accessed=3 << 20, transcendentals=0),
        name="finish",
    )(moved, moved)


def local(traces, coords, wavenumbers, fold, selected):
    sent = dft(traces[0])
    moved = lax.all_to_all(sent, "freq", split_axis=0, concat_axis=0, tiled=True)
    both = twice(moved)
    moved = lax.all_to_all(both, TRACE, split_axis=0, concat_axis=0, tiled=True)
    early = make_atoms(wavenumbers, coords, 0, EARLY)
    late = make_atoms(wavenumbers, coords, EARLY, 2048 - EARLY)
    cosine, sine, cross = chosen_tables(coords, wavenumbers, selected, fold)
    sent = pursue(moved.reshape(SLOTS, 256), cosine, sine, cross, fold, [early, late])
    moved = lax.all_to_all(sent, EIGHT, split_axis=0, concat_axis=0, tiled=True)
    spectrum, coefficients = finish(moved)
    return spectrum.reshape(256, 8, 2, 128), coefficients.reshape(2, 8, 2, 128)


def solution(mesh):
    split = Mesh(mesh.devices.reshape(8, 2, 2, 4), ("freq",) + TRACE)
    return jax.shard_map(
        local,
        mesh=split,
        in_specs=(P("freq", TRACE, None), P(), P(), P(), P(None, None, "freq")),
        out_specs=(P(TRACE, None, None, "freq"), P(None, None, None, "freq")),
        check_vma=False,
    )
```
